512 devices in a mesh: row: 16 (over y, x), col: 32 (over z, core).
Axes of the slice: x: 4, y: 4, z: 16, core: 2. Of those that a mesh axis runs over, the one named last changes fastest.
Arguments:
- momentum: float32 [4096, 14336], P('row', 'col'), may hold values from -6 to 6
- grads: bfloat16 [1, 4096, 14336], P(None, 'row', 'col'), may hold values from -6 to 6
- right_factor: float32 [128, 14336], P(None, 'col'), may hold values from -0.046875 to 0.046875
Outputs:
- new_momentum: float32 [4096, 14336], P('row', 'col')
- new_factor: float32 [128, 14336], P(None, 'col')
- update: float32 [4096, 14336], P('row', 'col')
The draws below stay inside these ranges and needn't reach their ends.
All inputs are finite; a program needn't handle non-finite values.
Results may differ from the reference program's by a relative error of at most 0.0005.
Values sent between devices are 32-bit elements; how exact they have to be, the bound alone decides.
A program may use at most 64 MiB of HBM per device.

```python
import jax
import jax.numpy as jnp
from jax import lax

M = 4096
N = 14336
RANK = 128
POWER = 2
STEPS = 1


def block_scale(rng, extent, shards, least, high):
    def one(axis_at, shards_of):
        steps = jax.random.uniform(jax.random.fold_in(jax.random.fold_in(rng, 6), axis_at), (shards_of,), jnp.float32, least / len(shards), high / len(shards))
        return jnp.repeat(jnp.exp(steps), extent[axis_at] // shards_of).reshape((-1,) + (1,) * (len(extent) - axis_at - 1))

    gain = one(*shards[0])
    for cut in shards[1:]:
        gain = gain * one(*cut)
    return gain


def bell_draw(key, dims, spread, reach, cuts=(), held_as=jnp.bfloat16):
    entries = spread * jax.random.normal(key, dims, jnp.float32)
    if cuts:
        entries = entries * block_scale(key, dims, cuts, -0.22, 0.18)
    return jnp.clip(entries, -reach, reach).astype(held_as)


def setup_inputs(seed: int = 0) -> dict:
    keys = jax.random.split(jax.random.key(seed), 4)
    return {
        "momentum": bell_draw(keys[0], (M, N), 1.0, 6.0, ((0, 16), (1, 32)), jnp.float32),
        "grads": bell_draw(keys[1], (STEPS, M, N), 1.0, 6.0, ((1, 16), (2, 32))),
        "right_factor": bell_draw(keys[2], (RANK, N), N ** -0.5, 0.046875, ((1, 32),), jnp.float32),
    }


DECAY_LEFT = 0.05
EPSILON = 1e-06

def contract(first, second, first_dim, second_dim):
    return lax.dot_general(first.astype(jnp.float32), second.astype(jnp.float32), (((first_dim,), (second_dim,)), ((), ())), precision=lax.Precision.HIGHEST, preferred_element_type=jnp.float32)

def reference(momentum, grads, right_factor):
    factor_t = right_factor
    moment = momentum
    accum = jnp.zeros(momentum.shape, jnp.float32)
    for step_index in range(STEPS):
        blend = moment + grads[step_index].astype(jnp.float32)
        for sweep_index in range(POWER):
            left_t = contract(factor_t, blend, 1, 1)
            gram_matrix = contract(left_t, left_t, 1, 1)
            lower_f = jnp.linalg.cholesky(gram_matrix)
            left_t = lax.linalg.triangular_solve(lower_f, left_t, left_side=True, lower=True)
            right_t = contract(left_t, blend, 1, 0)
            squares = lax.optimization_barrier(jnp.sum(right_t * right_t, axis=1, keepdims=True))
            factor_t = right_t / (jnp.sqrt(squares) + EPSILON)
        moment = blend - DECAY_LEFT * contract(left_t, right_t, 0, 0)
        accum = accum + contract(left_t, factor_t, 0, 0)
    return (moment, factor_t, accum * jnp.float32((M * N / RANK) ** 0.5))
```

```python
import jax
import jax.numpy as jnp
from jax import lax
from jax.experimental import pallas as pl
from jax.experimental.pallas import tpu as pltpu
from jax.sharding import PartitionSpec as P

M = 4096
N = 14336
RANK = 128
POWER = 2

DECAY_LEFT = 0.05
EPSILON = 1e-06
SCALE = (M * N / RANK) ** 0.5

ROWS = 16
COLS = 32
HIGH = 256
WIDE = 448
MESH = pl.DeviceIdType.MESH

TURNS = sorted(
    ((dy, dx) for dy in range(4) for dx in range(4) if dy or dx),
    key=lambda turn: -(min(turn[0], 4 - turn[0]) + min(turn[1], 4 - turn[1])),
)


def contract(first, second, first_dim, second_dim):
    return lax.dot_general(
        first,
        second,
        (((first_dim,), (second_dim,)), ((), ())),
        precision=lax.Precision.HIGHEST,
        preferred_element_type=jnp.float32,
    )


def spread(x):
    return jnp.broadcast_to(x, (8, 128))

def inverse_factor(w):
    lane = lax.broadcasted_iota(jnp.int32, (8, 128), 1)
    sub = lax.broadcasted_iota(jnp.int32, (8, 128), 0)
    for k in range(16):
        base = 8 * k
        tile = w[base:base + 8, :]
        inside = (lane >= base) & (lane < base + 8)
        column = [spread(tile[:, base + t:base + t + 1]) for t in range(8)]
        d = {(i, t): spread(column[t][i:i + 1, :]) for t in range(8) for i in range(t, 8)}
        start = jnp.where(inside, jnp.where(lane - base == sub, 1.0, 0.0), tile)
        rows = [spread(start[i:i + 1, :]) for i in range(8)]
        low, scale = {}, []
        for t in range(8):
            inv = lax.rsqrt(d[t, t])
            scale.append(inv)
            for i in range(t + 1, 8):
                low[i, t] = d[i, t] * inv
            rows[t] = rows[t] * inv
            for i in range(t + 1, 8):
                for j in range(t + 1, i + 1):
                    d[i, j] = d[i, j] - low[i, t] * low[j, t]
                rows[i] = rows[i] - low[i, t] * rows[t]
        block = rows[0]
        for t in range(1, 8):
            block = jnp.where(sub == t, rows[t], block)
        w[base:base + 8, :] = jnp.where(lane < base + 8, block, 0.0)
        if k == 15:
            break
        turned = block.T if k < 14 else None
        for kk in range(k + 1, 16):
            at = 8 * kk
            tile = w[at:at + 8, :]
            if kk == k + 1:
                ls = []
                for t in range(8):
                    x = spread(tile[:, base + t:base + t + 1])
                    for s in range(t):
                        x = x - ls[s] * low[t, s]
                    ls.append(x * scale[t])
            else:
                ls = [spread(turned[at:at + 8, t:t + 1]) for t in range(8)]
            tile = jnp.where(inside, 0.0, tile)
            for t in range(8):
                tile = tile - ls[t] * rows[t]
            w[at:at + 8, :] = tile


def kernel(
    momentum, grads, factor_in, new_momentum, new_factor, update,
    moment_v, grads_v, blend, right, left_part, left_got, left_t,
    gram_part, gram_got, gram, right_part, right_got, right_sum,
    square_own, square_got, factor_v, update_v,
    in_sem, out_sem, left_send, left_recv, gram_send, gram_recv,
    right_send, right_recv, square_send, square_recv,
):
    row = lax.axis_index("row")
    col = lax.axis_index("col")
    y, x = row // 4, row % 4

    col_peers = [(col + 16 + (k + 1) // 2 * (1 if k % 2 else -1) + COLS) % COLS for k in range(31)]
    row_peers = [(y + dy) % 4 * 4 + (x + dx) % 4 for dy, dx in TURNS]

    barrier = pltpu.get_barrier_semaphore()
    for peer in col_peers:
        pl.semaphore_signal(barrier, inc=1, device_id=(row, peer), device_id_type=MESH)
    for peer in row_peers:
        pl.semaphore_signal(barrier, inc=1, device_id=(peer, col), device_id_type=MESH)

    loads = [
        pltpu.make_async_copy(factor_in, right, in_sem.at[0]),
        pltpu.make_async_copy(momentum, moment_v, in_sem.at[1]),
        pltpu.make_async_copy(grads.at[0], grads_v, in_sem.at[2]),
    ]
    for load in loads:
        load.start()
    for load in loads:
        load.wait()
    blend[...] = moment_v[...] + grads_v[...].astype(jnp.float32)

    def remote(src, dst, send, recv, device):
        pltpu.make_async_remote_copy(
            src_ref=src, dst_ref=dst, send_sem=send, recv_sem=recv,
            device_id=device, device_id_type=MESH,
        ).start()

    def await_bytes(ref, sem):
        pltpu.make_async_copy(ref, ref, sem).wait()

    own_col = pl.ds(pl.multiple_of(8 * col, 8), 8)
    own_row = pl.ds(pl.multiple_of(8 * row, 8), 8)

    def sweep(step, carry):
        left_part[step] = contract(blend[...], right[...], 1, 1)

        @pl.when(step == 0)
        def _():
            pl.semaphore_wait(barrier, 46)

        for peer in col_peers:
            part = left_part.at[step, pl.ds(pl.multiple_of(8 * peer, 8), 8)]
            remote(part, left_got.at[step, col], left_send.at[step, 0], left_recv.at[step, 0], (row, peer))
        left_got[step, col] = left_part[step, own_col]
        await_bytes(left_got.at[step, pl.ds(0, COLS - 1)], left_recv.at[step, 0])
        left_t[step, own_col] = jnp.sum(left_got[step], axis=0)
        for peer in col_peers:
            mine = left_t.at[step, own_col]
            remote(mine, mine, left_send.at[step, 1], left_recv.at[step, 1], (row, peer))
        await_bytes(left_t.at[step, pl.ds(0, HIGH - 8)], left_recv.at[step, 1])

        gram_part[step] = contract(left_t[step], left_t[step], 0, 0)
        for peer in row_peers:
            part = gram_part.at[step, pl.ds(pl.multiple_of(8 * peer, 8), 8)]
            remote(part, gram_got.at[step, row], gram_send.at[step, 0], gram_recv.at[step, 0], (peer, col))
        right_part[step] = contract(left_t[step], blend[...], 0, 0)
        for peer in row_peers:
            part = right_part.at[step, pl.ds(pl.multiple_of(8 * peer, 8), 8)]
            remote(part, right_got.at[step, row], right_send.at[step, 0], right_recv.at[step, 0], (peer, col))

        gram_got[step, row] = gram_part[step, own_row]
        await_bytes(gram_got.at[step, pl.ds(0, ROWS - 1)], gram_recv.at[step, 0])
        gram[step, own_row] = jnp.sum(gram_got[step], axis=0)
        for peer in row_peers:
            mine = gram.at[step, own_row]
            remote(mine, mine, gram_send.at[step, 1], gram_recv.at[step, 1], (peer, col))
        right_got[step, row] = right_part[step, own_row]
        await_bytes(right_got.at[step, pl.ds(0, ROWS - 1)], right_recv.at[step, 0])
        right_sum[step, own_row] = jnp.sum(right_got[step], axis=0)
        for peer in row_peers:
            mine = right_sum.at[step, own_row]
            remote(mine, mine, right_send.at[step, 1], right_recv.at[step, 1], (peer, col))

        await_bytes(gram.at[step, pl.ds(0, RANK - 8)], gram_recv.at[step, 1])
        await_bytes(gram_got.at[step, pl.ds(0, ROWS - 1)], gram_send.at[step, 0])
        await_bytes(gram.at[step, pl.ds(0, RANK - 8)], gram_send.at[step, 1])
        inverse_factor(gram.at[step])
        await_bytes(right_sum.at[step, pl.ds(0, RANK - 8)], right_recv.at[step, 1])
        right[...] = contract(gram[step], right_sum[step], 1, 0)
        return carry

    lax.fori_loop(0, POWER, sweep, 0)
    last = POWER - 1

    square_own[...] = contract(jnp.ones((8, WIDE), jnp.float32), right[...] * right[...], 1, 1)[:1]
    square_got[col] = square_own[...]
    for peer in col_peers:
        remote(square_own, square_got.at[col], square_send, square_recv, (row, peer))
    left = contract(left_t[last], gram[last], 1, 1)
    moment_v[...] = blend[...] - DECAY_LEFT * contract(left, right[...], 1, 0)
    store = pltpu.make_async_copy(moment_v, new_momentum, out_sem.at[0])
    store.start()
    await_bytes(square_got.at[pl.ds(0, COLS - 1)], square_recv)
    norm = 1.0 / (jnp.sqrt(jnp.sum(square_got[...], axis=0)) + EPSILON)
    update_v[...] = contract(left * (norm * SCALE), right[...], 1, 0)
    store_update = pltpu.make_async_copy(update_v, update, out_sem.at[1])
    store_update.start()
    spot = lax.broadcasted_iota(jnp.int32, (RANK, RANK), 0) == lax.broadcasted_iota(jnp.int32, (RANK, RANK), 1)
    tall = jnp.sum(jnp.where(spot, jnp.broadcast_to(norm, (RANK, RANK)), 0.0), axis=1, keepdims=True)
    factor_v[...] = right[...] * tall
    store_factor = pltpu.make_async_copy(factor_v, new_factor, out_sem.at[2])
    store_factor.start()

    for step in range(POWER):
        await_bytes(left_got.at[step, pl.ds(0, COLS - 1)], left_send.at[step, 0])
        await_bytes(left_t.at[step, pl.ds(0, HIGH - 8)], left_send.at[step, 1])
        await_bytes(right_got.at[step, pl.ds(0, ROWS - 1)], right_send.at[step, 0])
        await_bytes(right_sum.at[step, pl.ds(0, RANK - 8)], right_send.at[step, 1])
    await_bytes(square_got.at[pl.ds(0, COLS - 1)], square_send)
    store.wait()
    store_update.wait()
    store_factor.wait()


def local(momentum, grads, right_factor):
    f32 = jnp.float32
    dma = pltpu.SemaphoreType.DMA
    return pl.pallas_call(
        kernel,
        out_shape=(
            jax.ShapeDtypeStruct((HIGH, WIDE), f32),
            jax.ShapeDtypeStruct((RANK, WIDE), f32),
            jax.ShapeDtypeStruct((HIGH, WIDE), f32),
        ),
        in_specs=[pl.BlockSpec(memory_space=pl.ANY)] * 3,
        out_specs=(pl.BlockSpec(memory_space=pl.ANY),) * 3,
        scratch_shapes=[
            pltpu.VMEM((HIGH, WIDE), f32),
            pltpu.VMEM((HIGH, WIDE), jnp.bfloat16),
            pltpu.VMEM((HIGH, WIDE), f32),
            pltpu.VMEM((RANK, WIDE), f32),
            pltpu.VMEM((POWER, HIGH, RANK), f32),
            pltpu.VMEM((POWER, COLS, 8, RANK), f32),
            pltpu.VMEM((POWER, HIGH, RANK), f32),
            pltpu.VMEM((POWER, RANK, RANK), f32),
            pltpu.VMEM((POWER, ROWS, 8, RANK), f32),
            pltpu.VMEM((POWER, RANK, RANK), f32),
            pltpu.VMEM((POWER, RANK, WIDE), f32),
            pltpu.VMEM((POWER, ROWS, 8, WIDE), f32),
            pltpu.VMEM((POWER, RANK, WIDE), f32),
            pltpu.VMEM((1, RANK), f32),
            pltpu.VMEM((COLS, 1, RANK), f32),
            pltpu.VMEM((RANK, WIDE), f32),
            pltpu.VMEM((HIGH, WIDE), f32),
            dma((3,)),
            dma((3,)),
            dma((POWER, 2)),
            dma((POWER, 2)),
            dma((POWER, 2)),
            dma((POWER, 2)),
            dma((POWER, 2)),
            dma((POWER, 2)),
            dma,
            dma,
        ],
        compiler_params=pltpu.CompilerParams(
            collective_id=0, has_side_effects=True, vmem_limit_bytes=16 << 20
        ),
    )(momentum, grads, right_factor)


def solution(mesh):
    return jax.shard_map(
        local,
        mesh=mesh,
        in_specs=(P("row", "col"), P(None, "row", "col"), P(None, "col")),
        out_specs=(P("row", "col"), P(None, "col"), P("row", "col")),
        check_vma=False,
    )
```

```python
import jax
import jax.numpy as jnp
from jax import lax
from jax.experimental import pallas as pl
from jax.experimental.pallas import tpu as pltpu
from jax.sharding import PartitionSpec as P

M = 4096
N = 14336
RANK = 128
POWER = 2

DECAY_LEFT = 0.05
EPSILON = 1e-06
SCALE = (M * N / RANK) ** 0.5

ROWS = 16
COLS = 32
HIGH = 256
WIDE = 448
SHARE = 32
OWNERS = WIDE // SHARE
GROUP = 8
MESH = pl.DeviceIdType.MESH

TURNS = sorted(
    ((dy, dx) for dy in range(4) for dx in range(4) if dy or dx),
    key=lambda turn: -(min(turn[0], 4 - turn[0]) + min(turn[1], 4 - turn[1])),
)


def contract(first, second, first_dim, second_dim):
    return lax.dot_general(
        first,
        second,
        (((first_dim,), (second_dim,)), ((), ())),
        precision=lax.Precision.HIGHEST,
        preferred_element_type=jnp.float32,
    )


def spread(x):
    return jnp.broadcast_to(x, (8, RANK))


def inverse_factor(w):
    lane = lax.broadcasted_iota(jnp.int32, (8, RANK), 1)
    sub = lax.broadcasted_iota(jnp.int32, (8, RANK), 0)
    count = RANK // 8
    tiles = [w[8 * i:8 * i + 8, :] for i in range(count)]
    for first in range(0, count, GROUP):
        stop = first + GROUP
        done, kept = [], []
        for k in range(first, stop):
            base = 8 * k
            tile = tiles[k]
            inside = (lane >= base) & (lane < base + 8)
            column = [spread(tile[:, base + t:base + t + 1]) for t in range(8)]
            d = {(i, t): spread(column[t][i:i + 1, :]) for t in range(8) for i in range(t, 8)}
            start = jnp.where(inside, jnp.where(lane - base == sub, 1.0, 0.0), tile)
            rows = [spread(start[i:i + 1, :]) for i in range(8)]
            low, scale = {}, []
            for t in range(8):
                inv = lax.rsqrt(d[t, t])
                scale.append(inv)
                for i in range(t + 1, 8):
                    low[i, t] = d[i, t] * inv
                rows[t] = rows[t] * inv
                for i in range(t + 1, 8):
                    for j in range(t + 1, i + 1):
                        d[i, j] = d[i, j] - low[i, t] * low[j, t]
                    rows[i] = rows[i] - low[i, t] * rows[t]
            block = rows[0]
            for t in range(1, 8):
                block = jnp.where(sub == t, rows[t], block)
            w[base:base + 8, :] = jnp.where(lane < base + 8, block, 0.0)
            done.append(block)
            kept.append(jnp.where((lane >= base + 8) & (lane < 8 * stop), 0.0, block))
            for kk in range(k + 1, stop):
                tile = tiles[kk]
                ls = []
                for t in range(8):
                    value = spread(tile[:, base + t:base + t + 1])
                    for s in range(t):
                        value = value - ls[s] * low[t, s]
                    ls.append(value * scale[t])
                tile = jnp.where(inside, 0.0, tile)
                for t in range(8):
                    tile = tile - ls[t] * rows[t]
                tiles[kk] = tile
        if stop < count:
            far = contract(jnp.concatenate(done, axis=0), jnp.concatenate(kept, axis=0), 0, 0)
            passed = (lane >= 8 * first) & (lane < 8 * stop)
            for kk in range(stop, count):
                tiles[kk] = jnp.where(passed, 0.0, tiles[kk]) - far[8 * kk:8 * kk + 8, :]


def kernel(
    momentum, grads, factor_in, moment_v, right, left_v, norm_v,
    grads_v, tall, blend, left_part, left_got, left_t,
    gram_part, gram_got, gram, right_part, right_got, right_sum,
    square_own, square_got, in_sem, left_send, left_recv, gram_send, gram_recv,
    right_send, right_recv, square_send, square_recv,
):
    row = lax.axis_index("row")
    col = lax.axis_index("col")
    y, x = row // 4, row % 4

    col_peers = [(col + 16 + (k + 1) // 2 * (1 if k % 2 else -1) + COLS) % COLS for k in range(31)]
    row_peers = [(y + dy) % 4 * 4 + (x + dx) % 4 for dy, dx in TURNS]

    barrier = pltpu.get_barrier_semaphore()
    for peer in col_peers:
        pl.semaphore_signal(barrier, inc=1, device_id=(row, peer), device_id_type=MESH)
    for peer in row_peers:
        pl.semaphore_signal(barrier, inc=1, device_id=(peer, col), device_id_type=MESH)

    loads = [
        pltpu.make_async_copy(momentum, moment_v, in_sem.at[1]),
        pltpu.make_async_copy(grads, grads_v, in_sem.at[2]),
        pltpu.make_async_copy(factor_in, right, in_sem.at[0]),
    ]
    for load in loads:
        load.start()
    for load in loads:
        load.wait()
    tall[...] = moment_v[...] + grads_v[...].astype(jnp.float32)
    blend[...] = tall[...].T

    def remote(src, dst, send, recv, device):
        pltpu.make_async_remote_copy(
            src_ref=src, dst_ref=dst, send_sem=send, recv_sem=recv,
            device_id=device, device_id_type=MESH,
        ).start()

    def await_bytes(ref, sem):
        pltpu.make_async_copy(ref, ref, sem).wait()

    own_col = pl.ds(pl.multiple_of(8 * col, 8), 8)
    own_row = pl.ds(pl.multiple_of(8 * row, 8), 8)

    def gathered(wait):
        @pl.when(row < OWNERS)
        def _():
            wait(WIDE - SHARE)

        @pl.when(row >= OWNERS)
        def _():
            wait(WIDE)

    def sweep(step, carry):
        left_part[step] = contract(blend[...], right[...], 1, 0)

        @pl.when(step == 0)
        def _():
            pl.semaphore_wait(barrier, 46)

        for peer in col_peers:
            part = left_part.at[step, pl.ds(pl.multiple_of(8 * peer, 8), 8)]
            remote(part, left_got.at[step, col], left_send.at[step, 0], left_recv.at[step, 0], (row, peer))
        left_got[step, col] = left_part[step, own_col]
        await_bytes(left_got.at[step, pl.ds(0, COLS - 1)], left_recv.at[step, 0])
        left_t[step, own_col] = jnp.sum(left_got[step], axis=0)
        for peer in col_peers:
            mine = left_t.at[step, own_col]
            remote(mine, mine, left_send.at[step, 1], left_recv.at[step, 1], (row, peer))
        await_bytes(left_t.at[step, pl.ds(0, HIGH - 8)], left_recv.at[step, 1])

        gram_part[step] = contract(left_t[step], left_t[step], 0, 0)
        for peer in row_peers:
            part = gram_part.at[step, pl.ds(pl.multiple_of(8 * peer, 8), 8)]
            remote(part, gram_got.at[step, row], gram_send.at[step, 0], gram_recv.at[step, 0], (peer, col))
        right_part[step] = contract(tall[...], left_t[step], 1, 0)
        for peer in row_peers:
            @pl.when(peer < OWNERS)
            def _():
                part = right_part.at[step, pl.ds(pl.multiple_of(SHARE * peer, SHARE), SHARE)]
                remote(part, right_got.at[step, row], right_send.at[step, 0], right_recv.at[step, 0], (peer, col))

        gram_got[step, row] = gram_part[step, own_row]
        await_bytes(gram_got.at[step, pl.ds(0, ROWS - 1)], gram_recv.at[step, 0])
        gram[step, own_row] = jnp.sum(gram_got[step], axis=0)
        for peer in row_peers:
            mine = gram.at[step, own_row]
            remote(mine, mine, gram_send.at[step, 1], gram_recv.at[step, 1], (peer, col))

        @pl.when(row < OWNERS)
        def _():
            share = pl.ds(pl.multiple_of(SHARE * row, SHARE), SHARE)
            right_got[step, row] = right_part[step, share]
            await_bytes(right_got.at[step, pl.ds(0, ROWS - 1)], right_recv.at[step, 0])
            right_sum[step, share] = jnp.sum(right_got[step], axis=0)
            for peer in row_peers:
                mine = right_sum.at[step, share]
                remote(mine, mine, right_send.at[step, 1], right_recv.at[step, 1], (peer, col))

        await_bytes(gram.at[step, pl.ds(0, RANK - 8)], gram_recv.at[step, 1])
        await_bytes(gram_got.at[step, pl.ds(0, ROWS - 1)], gram_send.at[step, 0])
        await_bytes(gram.at[step, pl.ds(0, RANK - 8)], gram_send.at[step, 1])
        inverse_factor(gram.at[step])
        gathered(lambda rows: await_bytes(right_sum.at[step, pl.ds(0, rows)], right_recv.at[step, 1]))
        right[...] = contract(right_sum[step], gram[step], 1, 1)
        return carry

    lax.fori_loop(0, POWER, sweep, 0)
    last = POWER - 1

    square_own[...] = jnp.sum(right[...] * right[...], axis=0, keepdims=True)
    square_got[col] = square_own[...]
    for peer in col_peers:
        remote(square_own, square_got.at[col], square_send, square_recv, (row, peer))
    left = contract(left_t[last], gram[last], 1, 1)
    moment_v[...] = tall[...] - DECAY_LEFT * contract(right[...], left, 1, 1)
    await_bytes(square_got.at[pl.ds(0, COLS - 1)], square_recv)
    norm = 1.0 / (jnp.sqrt(jnp.sum(square_got[...], axis=0)) + EPSILON)
    norm_v[...] = norm
    left_v[...] = left * (norm * SCALE)

    for step in range(POWER):
        await_bytes(left_got.at[step, pl.ds(0, COLS - 1)], left_send.at[step, 0])
        await_bytes(left_t.at[step, pl.ds(0, HIGH - 8)], left_send.at[step, 1])
        gathered(lambda rows: await_bytes(right_sum.at[step, pl.ds(0, rows)], right_send.at[step, 0]))

        @pl.when(row < OWNERS)
        def _():
            await_bytes(right_got.at[step, pl.ds(0, ROWS - 1)], right_send.at[step, 1])

    await_bytes(square_got.at[pl.ds(0, COLS - 1)], square_send)


def finish(moment, right, left, norm, new_momentum, new_factor, update, factor_v, update_v, out_sem):
    stores = [pltpu.make_async_copy(moment, new_momentum, out_sem.at[0])]
    stores[0].start()
    piece = WIDE // 4
    for k in range(4):
        rows = pl.ds(k * piece, piece)
        update_v[rows, :] = contract(right[rows, :], left[...], 1, 1)
        stores.append(pltpu.make_async_copy(update_v.at[rows], update.at[rows], out_sem.at[k + 1]))
        stores[-1].start()
    factor_v[...] = right[...] * norm[...]
    stores.append(pltpu.make_async_copy(factor_v, new_factor, out_sem.at[5]))
    stores[-1].start()
    for store in stores:
        store.wait()


def local(momentum, grads, right_factor):
    f32 = jnp.float32
    dma = pltpu.SemaphoreType.DMA
    passed = pl.pallas_call(
        kernel,
        out_shape=(
            jax.ShapeDtypeStruct((WIDE, HIGH), f32),
            jax.ShapeDtypeStruct((WIDE, RANK), f32),
            jax.ShapeDtypeStruct((HIGH, RANK), f32),
            jax.ShapeDtypeStruct((1, RANK), f32),
        ),
        in_specs=[pl.BlockSpec(memory_space=pltpu.HBM)] * 3,
        out_specs=(pl.BlockSpec(memory_space=pltpu.VMEM),) * 4,
        scratch_shapes=[
            pltpu.VMEM((WIDE, HIGH), jnp.bfloat16),
            pltpu.VMEM((WIDE, HIGH), f32),
            pltpu.VMEM((HIGH, WIDE), f32),
            pltpu.VMEM((POWER, HIGH, RANK), f32),
            pltpu.VMEM((POWER, COLS, 8, RANK), f32),
            pltpu.VMEM((POWER, HIGH, RANK), f32),
            pltpu.VMEM((POWER, RANK, RANK), f32),
            pltpu.VMEM((POWER, ROWS, 8, RANK), f32),
            pltpu.VMEM((POWER, RANK, RANK), f32),
            pltpu.VMEM((POWER, WIDE, RANK), f32),
            pltpu.VMEM((POWER, ROWS, SHARE, RANK), f32),
            pltpu.VMEM((POWER, WIDE, RANK), f32),
            pltpu.VMEM((1, RANK), f32),
            pltpu.VMEM((COLS, 1, RANK), f32),
            dma((3,)),
            dma((POWER, 2)),
            dma((POWER, 2)),
            dma((POWER, 2)),
            dma((POWER, 2)),
            dma((POWER, 2)),
            dma((POWER, 2)),
            dma,
            dma,
        ],
        compiler_params=pltpu.CompilerParams(
            collective_id=0, has_side_effects=True, vmem_limit_bytes=16 << 20
        ),
    )(*(pltpu.with_memory_space_constraint(given, pltpu.HBM) for given in (momentum.T, grads[0].T, right_factor.T)))
    outs = pl.pallas_call(
        finish,
        out_shape=(
            jax.ShapeDtypeStruct((WIDE, HIGH), f32),
            jax.ShapeDtypeStruct((WIDE, RANK), f32),
            jax.ShapeDtypeStruct((WIDE, HIGH), f32),
        ),
        in_specs=[pl.BlockSpec(memory_space=pltpu.VMEM)] * 4,
        out_specs=(pl.BlockSpec(memory_space=pltpu.HBM),) * 3,
        scratch_shapes=[pltpu.VMEM((WIDE, RANK), f32), pltpu.VMEM((WIDE, HIGH), f32), dma((6,))],
        compiler_params=pltpu.CompilerParams(vmem_limit_bytes=16 << 20),
    )(*passed)
    return tuple(out.T for out in outs)


def solution(mesh):
    return jax.shard_map(
        local,
        mesh=mesh,
        in_specs=(P("row", "col"), P(None, "row", "col"), P(None, "col")),
        out_specs=(P("row", "col"), P(None, "col"), P("row", "col")),
        check_vma=False,
    )
```

```python
import jax
import jax.numpy as jnp
from jax import lax
from jax.experimental import pallas as pl
from jax.experimental.pallas import tpu as pltpu
from jax.sharding import PartitionSpec as P

M = 4096
N = 14336
RANK = 128
POWER = 2

DECAY_LEFT = 0.05
EPSILON = 1e-06
SCALE = (M * N / RANK) ** 0.5

ROWS = 16
COLS = 32
CHIPS = 16
HIGH = 256
HALF = 128
NEAR = 5
WIDE = 448
SHARE = 32
OWNERS = WIDE // SHARE
GROUP = 8
MESH = pl.DeviceIdType.MESH

HOPS = sorted((hop for hop in range(1 - CHIPS // 2, CHIPS // 2 + 1) if hop), key=lambda hop: -abs(hop))

TURNS = sorted(
    ((dy, dx) for dy in range(4) for dx in range(4) if dy or dx),
    key=lambda turn: -(min(turn[0], 4 - turn[0]) + min(turn[1], 4 - turn[1])),
)


def contract(first, second, first_dim, second_dim):
    return lax.dot_general(
        first,
        second,
        (((first_dim,), (second_dim,)), ((), ())),
        precision=lax.Precision.HIGHEST,
        preferred_element_type=jnp.float32,
    )


def spread(x):
    return jnp.broadcast_to(x, (8, RANK))


def inverse_factor(w):
    lane = lax.broadcasted_iota(jnp.int32, (8, RANK), 1)
    sub = lax.broadcasted_iota(jnp.int32, (8, RANK), 0)
    count = RANK // 8
    tiles = [w[8 * i:8 * i + 8, :] for i in range(count)]
    for first in range(0, count, GROUP):
        stop = first + GROUP
        done, kept = [], []
        for k in range(first, stop):
            base = 8 * k
            tile = tiles[k]
            inside = (lane >= base) & (lane < base + 8)
            column = [spread(tile[:, base + t:base + t + 1]) for t in range(8)]
            d = {(i, t): spread(column[t][i:i + 1, :]) for t in range(8) for i in range(t, 8)}
            start = jnp.where(inside, jnp.where(lane - base == sub, 1.0, 0.0), tile)
            rows = [spread(start[i:i + 1, :]) for i in range(8)]
            low, scale = {}, []
            for t in range(8):
                inv = lax.rsqrt(d[t, t])
                scale.append(inv)
                for i in range(t + 1, 8):
                    low[i, t] = d[i, t] * inv
                rows[t] = rows[t] * inv
                for i in range(t + 1, 8):
                    for j in range(t + 1, i + 1):
                        d[i, j] = d[i, j] - low[i, t] * low[j, t]
                    rows[i] = rows[i] - low[i, t] * rows[t]
            block = rows[0]
            for t in range(1, 8):
                block = jnp.where(sub == t, rows[t], block)
            w[base:base + 8, :] = jnp.where(lane < base + 8, block, 0.0)
            done.append(block)
            kept.append(jnp.where((lane >= base + 8) & (lane < 8 * stop), 0.0, block))
            for kk in range(k + 1, stop):
                tile = tiles[kk]
                ls = []
                for t in range(8):
                    value = spread(tile[:, base + t:base + t + 1])
                    for s in range(t):
                        value = value - ls[s] * low[t, s]
                    ls.append(value * scale[t])
                tile = jnp.where(inside, 0.0, tile)
                for t in range(8):
                    tile = tile - ls[t] * rows[t]
                tiles[kk] = tile
        if stop < count:
            far = contract(jnp.concatenate(done, axis=0), jnp.concatenate(kept, axis=0), 0, 0)
            passed = (lane >= 8 * first) & (lane < 8 * stop)
            for kk in range(stop, count):
                tiles[kk] = jnp.where(passed, 0.0, tiles[kk]) - far[8 * kk:8 * kk + 8, :]


def kernel(
    momentum, grads, factor_in, moment_v, right, left_v, norm_v,
    grads_v, tall, blend, half_out, half_own, half_got, left_part, left_got, left_t,
    gram_part, gram_got, gram, right_part, right_got, right_sum,
    square_own, square_got, in_sem, pair_send, pair_recv, left_send, left_recv, gram_send, gram_recv,
    right_send, right_recv, square_send, square_recv,
):
    row = lax.axis_index("row")
    col = lax.axis_index("col")
    y, x = row // 4, row % 4
    z, core = col // 2, col % 2
    partner = (row, col + 1 - 2 * core)

    col_peers = [(col + 16 + (k + 1) // 2 * (1 if k % 2 else -1) + COLS) % COLS for k in range(31)]
    chips = [(hop, (z + hop + CHIPS) % CHIPS) for hop in HOPS]
    row_peers = [(y + dy) % 4 * 4 + (x + dx) % 4 for dy, dx in TURNS]

    barrier = pltpu.get_barrier_semaphore()
    for peer in col_peers:
        pl.semaphore_signal(barrier, inc=1, device_id=(row, peer), device_id_type=MESH)
    for peer in row_peers:
        pl.semaphore_signal(barrier, inc=1, device_id=(peer, col), device_id_type=MESH)

    loads = [
        pltpu.make_async_copy(momentum, moment_v, in_sem.at[1]),
        pltpu.make_async_copy(grads, grads_v, in_sem.at[2]),
        pltpu.make_async_copy(factor_in, right, in_sem.at[0]),
    ]
    for load in loads:
        load.start()
    for load in loads:
        load.wait()
    tall[...] = moment_v[...] + grads_v[...].astype(jnp.float32)
    blend[...] = tall[...].T

    def remote(src, dst, send, recv, device):
        pltpu.make_async_remote_copy(
            src_ref=src, dst_ref=dst, send_sem=send, recv_sem=recv,
            device_id=device, device_id_type=MESH,
        ).start()

    def await_bytes(ref, sem):
        pltpu.make_async_copy(ref, ref, sem).wait()

    ours = pl.multiple_of(HALF * core, HALF)
    theirs = pl.multiple_of(HALF * (1 - core), HALF)

    def piece(first, chip):
        return pl.ds(pl.multiple_of(first + 8 * chip, 8), 8)

    own_row = pl.ds(pl.multiple_of(8 * row, 8), 8)

    def gathered(wait):
        @pl.when(row < OWNERS)
        def _():
            wait(WIDE - SHARE)

        @pl.when(row >= OWNERS)
        def _():
            wait(WIDE)

    last = POWER - 1

    def sweep(step, carry):
        half_out[step] = contract(blend[pl.ds(theirs, HALF), :], right[...], 1, 0)

        @pl.when(step == 0)
        def _():
            pl.semaphore_wait(barrier, 46)

        remote(half_out.at[step], half_got.at[step], pair_send.at[step, 0], pair_recv.at[step, 0], partner)
        half_own[...] = contract(blend[pl.ds(ours, HALF), :], right[...], 1, 0)
        await_bytes(half_got.at[step], pair_recv.at[step, 0])
        left_part[step] = half_own[...] + half_got[step]
        for hop, chip in chips:
            part = left_part.at[step, piece(0, chip)]
            remote(part, left_got.at[step, z], left_send.at[step, 0], left_recv.at[step, 0], (row, 2 * chip + core))
        left_got[step, z] = left_part[step, piece(0, z)]
        await_bytes(left_got.at[step, pl.ds(0, CHIPS - 1)], left_recv.at[step, 0])
        left_t[step, piece(ours, z)] = jnp.sum(left_got[step], axis=0)
        mine = left_t.at[step, piece(ours, z)]
        for hop, chip in chips:
            arrival = left_recv.at[step, 1 if abs(hop) <= NEAR else 2]
            remote(mine, mine, left_send.at[step, 1], arrival, (row, 2 * chip + core))

        def forward(chip):
            part = left_t.at[step, piece(ours, chip)]
            remote(part, part, pair_send.at[step, 1], pair_recv.at[step, 1], partner)

        forward(z)
        near = [chip for hop, chip in chips if abs(hop) <= NEAR]
        far = [chip for hop, chip in chips if abs(hop) > NEAR]
        await_bytes(left_t.at[step, pl.ds(0, 8 * len(near))], left_recv.at[step, 1])
        for chip in near:
            forward(chip)
        await_bytes(left_t.at[step, pl.ds(0, 8 * len(far))], left_recv.at[step, 2])
        for chip in far:
            forward(chip)
        await_bytes(left_t.at[step, pl.ds(0, HALF)], pair_recv.at[step, 1])

        gram_part[step] = contract(left_t[step], left_t[step], 0, 0)
        for peer in row_peers:
            part = gram_part.at[step, pl.ds(pl.multiple_of(8 * peer, 8), 8)]
            remote(part, gram_got.at[step, row], gram_send.at[step, 0], gram_recv.at[step, 0], (peer, col))
        right_part[step] = contract(tall[...], left_t[step], 1, 0)
        for peer in row_peers:
            @pl.when(peer < OWNERS)
            def _():
                part = right_part.at[step, pl.ds(pl.multiple_of(SHARE * peer, SHARE), SHARE)]
                remote(part, right_got.at[step, row], right_send.at[step, 0], right_recv.at[step, 0], (peer, col))

        gram_got[step, row] = gram_part[step, own_row]
        await_bytes(gram_got.at[step, pl.ds(0, ROWS - 1)], gram_recv.at[step, 0])
        gram[step, own_row] = jnp.sum(gram_got[step], axis=0)
        for peer in row_peers:
            mine = gram.at[step, own_row]
            remote(mine, mine, gram_send.at[step, 1], gram_recv.at[step, 1], (peer, col))

        @pl.when(row < OWNERS)
        def _():
            share = pl.ds(pl.multiple_of(SHARE * row, SHARE), SHARE)
            right_got[step, row] = right_part[step, share]
            await_bytes(right_got.at[step, pl.ds(0, ROWS - 1)], right_recv.at[step, 0])
            right_sum[step, share] = jnp.sum(right_got[step], axis=0)
            for peer in row_peers:
                mine = right_sum.at[step, share]
                remote(mine, mine, right_send.at[step, 1], right_recv.at[step, 1], (peer, col))

        await_bytes(gram.at[step, pl.ds(0, RANK - 8)], gram_recv.at[step, 1])
        await_bytes(gram_got.at[step, pl.ds(0, ROWS - 1)], gram_send.at[step, 0])
        await_bytes(gram.at[step, pl.ds(0, RANK - 8)], gram_send.at[step, 1])
        inverse_factor(gram.at[step])
        gathered(lambda rows: await_bytes(right_sum.at[step, pl.ds(0, rows)], right_recv.at[step, 1]))
        spot = lax.broadcasted_iota(jnp.int32, (RANK, RANK), 0) == lax.broadcasted_iota(jnp.int32, (RANK, RANK), 1)
        weight = jnp.sqrt(jnp.sum(jnp.where(spot, gram[step], 0.0), axis=0, keepdims=True))
        right[...] = contract(right_sum[step], gram[step], 1, 1) * jnp.where(step < last, weight, 1.0)
        return carry

    lax.fori_loop(0, POWER, sweep, 0)
    square_own[...] = jnp.sum(right[...] * right[...], axis=0, keepdims=True)
    square_got[col] = square_own[...]
    for peer in col_peers:
        remote(square_own, square_got.at[col], square_send, square_recv, (row, peer))
    left = contract(left_t[last], gram[last], 1, 1)
    moment_v[...] = tall[...] - DECAY_LEFT * contract(right[...], left, 1, 1)
    await_bytes(square_got.at[pl.ds(0, COLS - 1)], square_recv)
    norm = 1.0 / (jnp.sqrt(jnp.sum(square_got[...], axis=0)) + EPSILON)
    norm_v[...] = norm
    left_v[...] = left * (norm * SCALE)

    for step in range(POWER):
        await_bytes(half_got.at[step], pair_send.at[step, 0])
        await_bytes(left_t.at[step, pl.ds(0, HALF)], pair_send.at[step, 1])
        await_bytes(left_got.at[step, pl.ds(0, CHIPS - 1)], left_send.at[step, 0])
        await_bytes(left_t.at[step, pl.ds(0, HALF - 8)], left_send.at[step, 1])
        gathered(lambda rows: await_bytes(right_sum.at[step, pl.ds(0, rows)], right_send.at[step, 0]))

        @pl.when(row < OWNERS)
        def _():
            await_bytes(right_got.at[step, pl.ds(0, ROWS - 1)], right_send.at[step, 1])

    await_bytes(square_got.at[pl.ds(0, COLS - 1)], square_send)


def finish(moment, right, left, norm, new_momentum, new_factor, update, factor_v, update_v, out_sem):
    stores = [pltpu.make_async_copy(moment, new_momentum, out_sem.at[0])]
    stores[0].start()
    piece = WIDE // 4
    for k in range(4):
        rows = pl.ds(k * piece, piece)
        update_v[rows, :] = contract(right[rows, :], left[...], 1, 1)
        stores.append(pltpu.make_async_copy(update_v.at[rows], update.at[rows], out_sem.at[k + 1]))
        stores[-1].start()
    factor_v[...] = right[...] * norm[...]
    stores.append(pltpu.make_async_copy(factor_v, new_factor, out_sem.at[5]))
    stores[-1].start()
    for store in stores:
        store.wait()


def local(momentum, grads, right_factor):
    f32 = jnp.float32
    dma = pltpu.SemaphoreType.DMA
    passed = pl.pallas_call(
        kernel,
        out_shape=(
            jax.ShapeDtypeStruct((WIDE, HIGH), f32),
            jax.ShapeDtypeStruct((WIDE, RANK), f32),
            jax.ShapeDtypeStruct((HIGH, RANK), f32),
            jax.ShapeDtypeStruct((1, RANK), f32),
        ),
        in_specs=[pl.BlockSpec(memory_space=pltpu.HBM)] * 3,
        out_specs=(pl.BlockSpec(memory_space=pltpu.VMEM),) * 4,
        scratch_shapes=[
            pltpu.VMEM((WIDE, HIGH), jnp.bfloat16),
            pltpu.VMEM((WIDE, HIGH), f32),
            pltpu.VMEM((HIGH, WIDE), f32),
            pltpu.VMEM((POWER, HALF, RANK), f32),
            pltpu.VMEM((HALF, RANK), f32),
            pltpu.VMEM((POWER, HALF, RANK), f32),
            pltpu.VMEM((POWER, HALF, RANK), f32),
            pltpu.VMEM((POWER, CHIPS, 8, RANK), f32),
            pltpu.VMEM((POWER, HIGH, RANK), f32),
            pltpu.VMEM((POWER, RANK, RANK), f32),
            pltpu.VMEM((POWER, ROWS, 8, RANK), f32),
            pltpu.VMEM((POWER, RANK, RANK), f32),
            pltpu.VMEM((POWER, WIDE, RANK), f32),
            pltpu.VMEM((POWER, ROWS, SHARE, RANK), f32),
            pltpu.VMEM((POWER, WIDE, RANK), f32),
            pltpu.VMEM((1, RANK), f32),
            pltpu.VMEM((COLS, 1, RANK), f32),
            dma((3,)),
            dma((POWER, 2)),
            dma((POWER, 2)),
            dma((POWER, 2)),
            dma((POWER, 3)),
            dma((POWER, 2)),
            dma((POWER, 2)),
            dma((POWER, 2)),
            dma((POWER, 2)),
            dma,
            dma,
        ],
        compiler_params=pltpu.CompilerParams(
            collective_id=0, has_side_effects=True, vmem_limit_bytes=16 << 20
        ),
    )(*(pltpu.with_memory_space_constraint(given, pltpu.HBM) for given in (momentum.T, grads[0].T, right_factor.T)))
    outs = pl.pallas_call(
        finish,
        out_shape=(
            jax.ShapeDtypeStruct((WIDE, HIGH), f32),
            jax.ShapeDtypeStruct((WIDE, RANK), f32),
            jax.ShapeDtypeStruct((WIDE, HIGH), f32),
        ),
        in_specs=[pl.BlockSpec(memory_space=pltpu.VMEM)] * 4,
        out_specs=(pl.BlockSpec(memory_space=pltpu.HBM),) * 3,
        scratch_shapes=[pltpu.VMEM((WIDE, RANK), f32), pltpu.VMEM((WIDE, HIGH), f32), dma((6,))],
        compiler_params=pltpu.CompilerParams(vmem_limit_bytes=16 << 20),
    )(*passed)
    return tuple(out.T for out in outs)


def solution(mesh):
    return jax.shard_map(
        local,
        mesh=mesh,
        in_specs=(P("row", "col"), P(None, "row", "col"), P(None, "col")),
        out_specs=(P("row", "col"), P(None, "col"), P("row", "col")),
        check_vma=False,
    )
```

```python
import jax
import jax.numpy as jnp
from jax import lax
from jax.experimental import pallas as pl
from jax.experimental.pallas import tpu as pltpu
from jax.sharding import PartitionSpec as P

M = 4096
N = 14336
RANK = 128
POWER = 2

DECAY_LEFT = 0.05
EPSILON = 1e-06
SCALE = (M * N / RANK) ** 0.5

ROWS = 16
COLS = 32
CHIPS = 16
HIGH = 256
HALF = 128
NEAR = 5
WIDE = 448
GROUP = 8
MESH = pl.DeviceIdType.MESH

HOPS = sorted((hop for hop in range(1 - CHIPS // 2, CHIPS // 2 + 1) if hop), key=lambda hop: -abs(hop))

TURNS = sorted(
    ((dy, dx) for dy in range(4) for dx in range(4) if dy or dx),
    key=lambda turn: -(min(turn[0], 4 - turn[0]) + min(turn[1], 4 - turn[1])),
)


def contract(first, second, first_dim, second_dim):
    return lax.dot_general(
        first,
        second,
        (((first_dim,), (second_dim,)), ((), ())),
        precision=lax.Precision.HIGHEST,
        preferred_element_type=jnp.float32,
    )


def spread(x):
    return jnp.broadcast_to(x, (8, RANK))


def inverse_factor(w, plain):
    lane = lax.broadcasted_iota(jnp.int32, (8, RANK), 1)
    sub = lax.broadcasted_iota(jnp.int32, (8, RANK), 0)
    count = RANK // 8
    tiles = [w[8 * i:8 * i + 8, :] for i in range(count)]
    for first in range(0, count, GROUP):
        stop = first + GROUP
        done, kept = [], []
        for k in range(first, stop):
            base = 8 * k
            tile = tiles[k]
            inside = (lane >= base) & (lane < base + 8)
            column = [jnp.where(sub >= 0, spread(tile[:, base + t:base + t + 1]), 0.0) for t in range(8)]
            d = {(i, t): spread(column[t][i:i + 1, :]) for t in range(8) for i in range(t, 8)}
            start = jnp.where(inside, jnp.where(lane - base == sub, 1.0, 0.0), tile)
            rows = [spread(start[i:i + 1, :]) for i in range(8)]
            low, scale = {}, []
            for t in range(8):
                inv = lax.rsqrt(d[t, t])
                scale.append(inv)
                for i in range(t + 1, 8):
                    low[i, t] = d[i, t] * inv
                rows[t] = rows[t] * inv
                for i in range(t + 1, 8):
                    for j in range(t + 1, i + 1):
                        d[i, j] = d[i, j] - low[i, t] * low[j, t]
                    rows[i] = rows[i] - low[i, t] * rows[t]
            block, factor = rows[0], scale[0]
            for t in range(1, 8):
                block = jnp.where(sub == t, rows[t], block)
                factor = jnp.where(sub == t, scale[t], factor)
            factor = jnp.where(plain, 1.0, jnp.sqrt(factor))
            w[base:base + 8, :] = jnp.where(lane < base + 8, block * factor, 0.0)
            done.append(block)
            kept.append(jnp.where((lane >= base + 8) & (lane < 8 * stop), 0.0, block))
            for kk in range(k + 1, stop):
                tile = tiles[kk]
                ls = []
                for t in range(8):
                    value = spread(tile[:, base + t:base + t + 1])
                    for s in range(t):
                        value = value - ls[s] * low[t, s]
                    ls.append(value * scale[t])
                tile = jnp.where(inside, 0.0, tile)
                for t in range(8):
                    tile = tile - ls[t] * rows[t]
                tiles[kk] = tile
        if stop < count:
            far = contract(jnp.concatenate(done, axis=0), jnp.concatenate(kept, axis=0), 0, 0)
            passed = (lane >= 8 * first) & (lane < 8 * stop)
            for kk in range(stop, count):
                tiles[kk] = jnp.where(passed, 0.0, tiles[kk]) - far[8 * kk:8 * kk + 8, :]


def kernel(
    momentum, grads, factor_in, moment, right_tall, left, norm,
    momentum_v, grads_v, factor_v, tall, blend, right,
    half_out, half_own, half_got, left_part, left_got, left_h,
    gram_part, gram_got, gram, right_part, right_got, right_sum, square_own, square_got,
    in_sem, pair_send, pair_recv, left_send, left_recv, gram_send, gram_recv,
    right_send, right_recv, square_send, square_recv,
):
    row = lax.axis_index("row")
    col = lax.axis_index("col")
    y, x = row // 4, row % 4
    z, core = col // 2, col % 2
    partner = (row, col + 1 - 2 * core)

    col_peers = [(col + 16 + (k + 1) // 2 * (1 if k % 2 else -1) + COLS) % COLS for k in range(31)]
    chips = [(hop, (z + hop + CHIPS) % CHIPS) for hop in HOPS]
    row_peers = [(y + dy) % 4 * 4 + (x + dx) % 4 for dy, dx in TURNS]

    barrier = pltpu.get_barrier_semaphore()
    for peer in col_peers:
        pl.semaphore_signal(barrier, inc=1, device_id=(row, peer), device_id_type=MESH)
    for peer in row_peers:
        pl.semaphore_signal(barrier, inc=1, device_id=(peer, col), device_id_type=MESH)

    loads = [
        pltpu.make_async_copy(momentum, momentum_v, in_sem.at[0]),
        pltpu.make_async_copy(grads, grads_v, in_sem.at[1]),
        pltpu.make_async_copy(factor_in, factor_v, in_sem.at[2]),
    ]
    for load in loads:
        load.start()
    for load in loads:
        load.wait()
    tall[...] = momentum_v[...] + grads_v[...].astype(jnp.float32)
    blend[...] = tall[...].T
    right[...] = factor_v[...].T

    def remote(src, dst, send, recv, device):
        pltpu.make_async_remote_copy(
            src_ref=src, dst_ref=dst, send_sem=send, recv_sem=recv,
            device_id=device, device_id_type=MESH,
        ).start()

    def await_bytes(ref, sem):
        pltpu.make_async_copy(ref, ref, sem).wait()

    def piece(place):
        return pl.ds(pl.multiple_of(8 * place, 8), 8)

    last = POWER - 1

    def sweep(step, carry):
        part = contract(right[...], tall[...], 1, 0)
        first, second = part[:, :HALF], part[:, HALF:]
        half_out[step] = jnp.where(core == 0, second, first)
        half_own[...] = jnp.where(core == 0, first, second)

        @pl.when(step == 0)
        def _():
            pl.semaphore_wait(barrier, 46)

        remote(half_out.at[step], half_got.at[step], pair_send.at[step, 0], pair_recv.at[step, 0], partner)
        await_bytes(half_got.at[step], pair_recv.at[step, 0])
        left_part[step] = half_own[...] + half_got[step]
        for hop, chip in chips:
            share = left_part.at[step, piece(chip)]
            remote(share, left_got.at[step, z], left_send.at[step, 0], left_recv.at[step, 0], (row, 2 * chip + core))
        left_got[step, z] = left_part[step, piece(z)]
        await_bytes(left_got.at[step, pl.ds(0, CHIPS - 1)], left_recv.at[step, 0])
        left_h[step, core, piece(z)] = jnp.sum(left_got[step], axis=0)
        mine = left_h.at[step, core, piece(z)]
        for hop, chip in chips:
            arrival = left_recv.at[step, 1 if abs(hop) <= NEAR else 2]
            remote(mine, mine, left_send.at[step, 1], arrival, (row, 2 * chip + core))

        def forward(chip):
            share = left_h.at[step, core, piece(chip)]
            remote(share, share, pair_send.at[step, 1], pair_recv.at[step, 1], partner)

        forward(z)
        near = [chip for hop, chip in chips if abs(hop) <= NEAR]
        far = [chip for hop, chip in chips if abs(hop) > NEAR]
        await_bytes(left_part.at[step, pl.ds(0, 8 * len(near))], left_recv.at[step, 1])
        for chip in near:
            forward(chip)
        await_bytes(left_part.at[step, pl.ds(0, 8 * len(far))], left_recv.at[step, 2])
        for chip in far:
            forward(chip)
        await_bytes(left_part.at[step], pair_recv.at[step, 1])

        raw = jnp.concatenate([left_h[step, 0], left_h[step, 1]], axis=1)
        gram_part[step] = contract(raw, raw, 1, 1)
        for peer in row_peers:
            share = gram_part.at[step, piece(peer)]
            remote(share, gram_got.at[step, row], gram_send.at[step, 0], gram_recv.at[step, 0], (peer, col))
        right_part[step] = contract(raw, blend[...], 1, 0)
        for peer in row_peers:
            share = right_part.at[step, piece(peer)]
            remote(share, right_got.at[step, row], right_send.at[step, 0], right_recv.at[step, 0], (peer, col))

        gram_got[step, row] = gram_part[step, piece(row)]
        await_bytes(gram_got.at[step, pl.ds(0, ROWS - 1)], gram_recv.at[step, 0])
        gram[step, piece(row)] = jnp.sum(gram_got[step], axis=0)
        for peer in row_peers:
            share = gram.at[step, piece(row)]
            remote(share, share, gram_send.at[step, 1], gram_recv.at[step, 1], (peer, col))
        right_got[step, row] = right_part[step, piece(row)]
        await_bytes(right_got.at[step, pl.ds(0, ROWS - 1)], right_recv.at[step, 0])
        right_sum[step, piece(row)] = jnp.sum(right_got[step], axis=0)
        for peer in row_peers:
            share = right_sum.at[step, piece(row)]
            remote(share, share, right_send.at[step, 1], right_recv.at[step, 1], (peer, col))

        await_bytes(gram.at[step, pl.ds(0, RANK - 8)], gram_recv.at[step, 1])
        await_bytes(gram_got.at[step, pl.ds(0, ROWS - 1)], gram_send.at[step, 0])
        await_bytes(gram.at[step, pl.ds(0, RANK - 8)], gram_send.at[step, 1])
        inverse_factor(gram.at[step], step == last)
        await_bytes(right_sum.at[step, pl.ds(0, RANK - 8)], right_recv.at[step, 1])
        right[...] = contract(gram[step], right_sum[step], 1, 0)
        return carry

    lax.fori_loop(0, POWER, sweep, 0)

    right_tall[...] = right[...].T
    square_own[...] = jnp.sum(right_tall[...] * right_tall[...], axis=0, keepdims=True)
    square_got[col] = square_own[...]
    for peer in col_peers:
        remote(square_own, square_got.at[col], square_send, square_recv, (row, peer))
    left[:, :HALF] = contract(gram[last], left_h[last, 0], 1, 0)
    left[:, HALF:] = contract(gram[last], left_h[last, 1], 1, 0)
    moment[...] = tall[...] - DECAY_LEFT * contract(right_tall[...], left[...], 1, 0)
    await_bytes(square_got.at[pl.ds(0, COLS - 1)], square_recv)
    norm[...] = 1.0 / (jnp.sqrt(jnp.sum(square_got[...], axis=0)) + EPSILON)

    for step in range(POWER):
        await_bytes(half_got.at[step], pair_send.at[step, 0])
        await_bytes(left_part.at[step], pair_send.at[step, 1])
        await_bytes(left_got.at[step, pl.ds(0, CHIPS - 1)], left_send.at[step, 0])
        await_bytes(left_part.at[step, pl.ds(0, HALF - 8)], left_send.at[step, 1])
        await_bytes(right_got.at[step, pl.ds(0, ROWS - 1)], right_send.at[step, 0])
        await_bytes(right_sum.at[step, pl.ds(0, RANK - 8)], right_send.at[step, 1])
    await_bytes(square_got.at[pl.ds(0, COLS - 1)], square_send)


def finish(moment, right_tall, left, norm, new_momentum, new_factor, update, factor_v, update_v, out_sem):
    stores = [pltpu.make_async_copy(moment, new_momentum, out_sem.at[0])]
    stores[0].start()
    factor_v[...] = right_tall[...] * norm[...]
    stores.append(pltpu.make_async_copy(factor_v, new_factor, out_sem.at[1]))
    stores[-1].start()
    span = WIDE // 4
    for k in range(4):
        rows = pl.ds(k * span, span)
        update_v[rows, :] = contract(factor_v[rows, :] * SCALE, left[...], 1, 0)
        stores.append(pltpu.make_async_copy(update_v.at[rows], update.at[rows], out_sem.at[k + 2]))
        stores[-1].start()
    for store in stores:
        store.wait()


def local(momentum, grads, right_factor):
    f32 = jnp.float32
    dma = pltpu.SemaphoreType.DMA
    given = (momentum.T, grads[0].T, right_factor.T)
    passed = pl.pallas_call(
        kernel,
        out_shape=(
            jax.ShapeDtypeStruct((WIDE, HIGH), f32),
            jax.ShapeDtypeStruct((WIDE, RANK), f32),
            jax.ShapeDtypeStruct((RANK, HIGH), f32),
            jax.ShapeDtypeStruct((1, RANK), f32),
        ),
        in_specs=[pl.BlockSpec(memory_space=pltpu.HBM)] * 3,
        out_specs=(pl.BlockSpec(memory_space=pltpu.VMEM),) * 4,
        scratch_shapes=[
            pltpu.VMEM((WIDE, HIGH), f32),
            pltpu.VMEM((WIDE, HIGH), jnp.bfloat16),
            pltpu.VMEM((WIDE, RANK), f32),
            pltpu.VMEM((WIDE, HIGH), f32),
            pltpu.VMEM((HIGH, WIDE), f32),
            pltpu.VMEM((RANK, WIDE), f32),
            pltpu.VMEM((POWER, RANK, HALF), f32),
            pltpu.VMEM((RANK, HALF), f32),
            pltpu.VMEM((POWER, RANK, HALF), f32),
            pltpu.VMEM((POWER, RANK, HALF), f32),
            pltpu.VMEM((POWER, CHIPS, 8, HALF), f32),
            pltpu.VMEM((POWER, 2, RANK, HALF), f32),
            pltpu.VMEM((POWER, RANK, RANK), f32),
            pltpu.VMEM((POWER, ROWS, 8, RANK), f32),
            pltpu.VMEM((POWER, RANK, RANK), f32),
            pltpu.VMEM((POWER, RANK, WIDE), f32),
            pltpu.VMEM((POWER, ROWS, 8, WIDE), f32),
            pltpu.VMEM((POWER, RANK, WIDE), f32),
            pltpu.VMEM((1, RANK), f32),
            pltpu.VMEM((COLS, 1, RANK), f32),
            dma((3,)),
            dma((POWER, 2)),
            dma((POWER, 2)),
            dma((POWER, 2)),
            dma((POWER, 3)),
            dma((POWER, 2)),
            dma((POWER, 2)),
            dma((POWER, 2)),
            dma((POWER, 2)),
            dma,
            dma,
        ],
        compiler_params=pltpu.CompilerParams(
            collective_id=0, has_side_effects=True, vmem_limit_bytes=16 << 20
        ),
    )(*(pltpu.with_memory_space_constraint(array, pltpu.HBM) for array in given))
    outs = pl.pallas_call(
        finish,
        out_shape=(
            jax.ShapeDtypeStruct((WIDE, HIGH), f32),
            jax.ShapeDtypeStruct((WIDE, RANK), f32),
            jax.ShapeDtypeStruct((WIDE, HIGH), f32),
        ),
        in_specs=[pl.BlockSpec(memory_space=pltpu.VMEM)] * 4,
        out_specs=(pl.BlockSpec(memory_space=pltpu.HBM),) * 3,
        scratch_shapes=[pltpu.VMEM((WIDE, RANK), f32), pltpu.VMEM((WIDE, HIGH), f32), dma((6,))],
        compiler_params=pltpu.CompilerParams(vmem_limit_bytes=16 << 20),
    )(*passed)
    return tuple(out.T for out in outs)


def solution(mesh):
    return jax.shard_map(
        local,
        mesh=mesh,
        in_specs=(P("row", "col"), P(None, "row", "col"), P(None, "col")),
        out_specs=(P("row", "col"), P(None, "col"), P("row", "col")),
        check_vma=False,
    )
```

```python
import jax
import jax.numpy as jnp
from jax import lax
from jax.experimental import pallas as pl
from jax.experimental.pallas import tpu as pltpu
from jax.sharding import PartitionSpec as P

M = 4096
N = 14336
RANK = 128
POWER = 2

DECAY_LEFT = 0.05
EPSILON = 1e-06
SCALE = (M * N / RANK) ** 0.5

ROWS = 16
COLS = 32
CHIPS = 16
HIGH = 256
HALF = 128
NEAR = 5
WIDE = 448
GROUP = 8
MESH = pl.DeviceIdType.MESH

HOPS = sorted((hop for hop in range(1 - CHIPS // 2, CHIPS // 2 + 1) if hop), key=lambda hop: -abs(hop))

TURNS = sorted(
    ((dy, dx) for dy in range(4) for dx in range(4) if dy or dx),
    key=lambda turn: -(min(turn[0], 4 - turn[0]) + min(turn[1], 4 - turn[1])),
)


def contract(first, second, first_dim, second_dim):
    return lax.dot_general(
        first,
        second,
        (((first_dim,), (second_dim,)), ((), ())),
        precision=lax.Precision.HIGHEST,
        preferred_element_type=jnp.float32,
    )


def spread(x):
    return jnp.broadcast_to(x, (8, RANK))


def inverse_factor(w, plain):
    lane = lax.broadcasted_iota(jnp.int32, (8, RANK), 1)
    sub = lax.broadcasted_iota(jnp.int32, (8, RANK), 0)
    count = RANK // 8
    tiles = [w[8 * i:8 * i + 8, :] for i in range(count)]
    for first in range(0, count, GROUP):
        stop = first + GROUP
        done, kept = [], []
        for k in range(first, stop):
            base = 8 * k
            tile = tiles[k]
            inside = (lane >= base) & (lane < base + 8)
            column = [jnp.where(sub >= 0, spread(tile[:, base + t:base + t + 1]), 0.0) for t in range(8)]
            d = {(i, t): spread(column[t][i:i + 1, :]) for t in range(8) for i in range(t, 8)}
            start = jnp.where(inside, jnp.where(lane - base == sub, 1.0, 0.0), tile)
            rows = [spread(start[i:i + 1, :]) for i in range(8)]
            low, scale = {}, []
            for t in range(8):
                inv = lax.rsqrt(d[t, t])
                scale.append(inv)
                for i in range(t + 1, 8):
                    low[i, t] = d[i, t] * inv
                rows[t] = rows[t] * inv
                for i in range(t + 1, 8):
                    for j in range(t + 1, i + 1):
                        d[i, j] = d[i, j] - low[i, t] * low[j, t]
                    rows[i] = rows[i] - low[i, t] * rows[t]
            block, factor = rows[0], scale[0]
            for t in range(1, 8):
                block = jnp.where(sub == t, rows[t], block)
                factor = jnp.where(sub == t, scale[t], factor)
            factor = jnp.where(plain, 1.0, jnp.sqrt(factor))
            w[base:base + 8, :] = jnp.where(lane < base + 8, block * factor, 0.0)
            done.append(block)
            kept.append(jnp.where((lane >= base + 8) & (lane < 8 * stop), 0.0, block))
            for kk in range(k + 1, stop):
                tile = tiles[kk]
                ls = []
                for t in range(8):
                    value = spread(tile[:, base + t:base + t + 1])
                    for s in range(t):
                        value = value - ls[s] * low[t, s]
                    ls.append(value * scale[t])
                tile = jnp.where(inside, 0.0, tile)
                for t in range(8):
                    tile = tile - ls[t] * rows[t]
                tiles[kk] = tile
        if stop < count:
            far = contract(jnp.concatenate(done, axis=0), jnp.concatenate(kept, axis=0), 0, 0)
            passed = (lane >= 8 * first) & (lane < 8 * stop)
            for kk in range(stop, count):
                tiles[kk] = jnp.where(passed, 0.0, tiles[kk]) - far[8 * kk:8 * kk + 8, :]


def kernel(
    momentum, grads, factor_in, moment, right_tall, left, norm,
    momentum_v, grads_v, factor_v, tall, blend, right,
    half_out, half_own, half_got, left_part, left_got, left_h,
    gram_part, gram_got, gram, right_part, right_got, right_sum, square_own, square_got,
    in_sem, pair_send, pair_recv, left_send, left_recv, gram_send, gram_recv,
    right_send, right_recv, square_send, square_recv,
):
    row = lax.axis_index("row")
    col = lax.axis_index("col")
    y, x = row // 4, row % 4
    z, core = col // 2, col % 2
    partner = (row, col + 1 - 2 * core)

    col_peers = [(col + 16 + (k + 1) // 2 * (1 if k % 2 else -1) + COLS) % COLS for k in range(31)]
    chips = [(hop, (z + hop + CHIPS) % CHIPS) for hop in HOPS]
    row_peers = [(y + dy) % 4 * 4 + (x + dx) % 4 for dy, dx in TURNS]

    barrier = pltpu.get_barrier_semaphore()
    for peer in col_peers:
        pl.semaphore_signal(barrier, inc=1, device_id=(row, peer), device_id_type=MESH)
    for peer in row_peers:
        pl.semaphore_signal(barrier, inc=1, device_id=(peer, col), device_id_type=MESH)
    for peer in row_peers:
        pl.semaphore_signal(barrier, inc=1, device_id=(peer, partner[1]), device_id_type=MESH)

    loads = [
        pltpu.make_async_copy(momentum, momentum_v, in_sem.at[0]),
        pltpu.make_async_copy(grads, grads_v, in_sem.at[1]),
        pltpu.make_async_copy(factor_in, factor_v, in_sem.at[2]),
    ]
    for load in loads:
        load.start()
    for load in loads:
        load.wait()
    tall[...] = momentum_v[...] + grads_v[...].astype(jnp.float32)
    right[...] = factor_v[...].T

    def remote(src, dst, send, recv, device):
        pltpu.make_async_remote_copy(
            src_ref=src, dst_ref=dst, send_sem=send, recv_sem=recv,
            device_id=device, device_id_type=MESH,
        ).start()

    def await_bytes(ref, sem):
        pltpu.make_async_copy(ref, ref, sem).wait()

    def piece(place):
        return pl.ds(pl.multiple_of(8 * place, 8), 8)

    owner = row % 2 == core
    last = POWER - 1

    def sweep(step, carry):
        part = contract(right[...], tall[...], 1, 0)
        first, second = part[:, :HALF], part[:, HALF:]
        half_out[step] = jnp.where(core == 0, second, first)
        half_own[...] = jnp.where(core == 0, first, second)

        @pl.when(step == 0)
        def _():
            pl.semaphore_wait(barrier, 61)

        remote(half_out.at[step], half_got.at[step], pair_send.at[step, 0], pair_recv.at[step, 0], partner)
        await_bytes(half_got.at[step], pair_recv.at[step, 0])
        left_part[step] = half_own[...] + half_got[step]
        for hop, chip in chips:
            share = left_part.at[step, piece(chip)]
            remote(share, left_got.at[step, z], left_send.at[step, 0], left_recv.at[step, 0], (row, 2 * chip + core))
        left_got[step, z] = left_part[step, piece(z)]

        @pl.when(step == 0)
        def _():
            blend[...] = tall[...].T

        await_bytes(left_got.at[step, pl.ds(0, CHIPS - 1)], left_recv.at[step, 0])
        left_h[step, core, piece(z)] = jnp.sum(left_got[step], axis=0)
        mine = left_h.at[step, core, piece(z)]
        for hop, chip in chips:
            arrival = left_recv.at[step, 1 if abs(hop) <= NEAR else 2]
            remote(mine, mine, left_send.at[step, 1], arrival, (row, 2 * chip + core))

        def forward(chip):
            share = left_h.at[step, core, piece(chip)]
            remote(share, share, pair_send.at[step, 1], pair_recv.at[step, 1], partner)

        forward(z)
        near = [chip for hop, chip in chips if abs(hop) <= NEAR]
        far = [chip for hop, chip in chips if abs(hop) > NEAR]
        await_bytes(left_part.at[step, pl.ds(0, 8 * len(near))], left_recv.at[step, 1])
        for chip in near:
            forward(chip)
        await_bytes(left_part.at[step, pl.ds(0, 8 * len(far))], left_recv.at[step, 2])
        for chip in far:
            forward(chip)
        await_bytes(left_part.at[step], pair_recv.at[step, 1])

        raw = jnp.concatenate([left_h[step, 0], left_h[step, 1]], axis=1)
        gram_part[step] = contract(raw, raw, 1, 1)
        for peer in row_peers:
            @pl.when(peer % 2 == core)
            def _():
                share = gram_part.at[step, piece(peer)]
                remote(share, gram_got.at[step, row], gram_send.at[step, 0], gram_recv.at[step, 0], (peer, col))

        right_part[step] = contract(raw, blend[...], 1, 0)
        for peer in row_peers:
            share = right_part.at[step, piece(peer)]
            remote(share, right_got.at[step, row], right_send.at[step, 0], right_recv.at[step, 0], (peer, col))

        @pl.when(owner)
        def _():
            gram_got[step, row] = gram_part[step, piece(row)]
            await_bytes(gram_got.at[step, pl.ds(0, ROWS - 1)], gram_recv.at[step, 0])
            gram[step, piece(row)] = jnp.sum(gram_got[step], axis=0)
            share = gram.at[step, piece(row)]
            for peer in row_peers:
                for side in (col, partner[1]):
                    remote(share, share, gram_send.at[step, 1], gram_recv.at[step, 1], (peer, side))
            remote(share, share, gram_send.at[step, 1], gram_recv.at[step, 1], partner)

        right_got[step, row] = right_part[step, piece(row)]
        await_bytes(right_got.at[step, pl.ds(0, ROWS - 1)], right_recv.at[step, 0])
        right_sum[step, piece(row)] = jnp.sum(right_got[step], axis=0)
        for peer in row_peers:
            share = right_sum.at[step, piece(row)]
            remote(share, share, right_send.at[step, 1], right_recv.at[step, 1], (peer, col))

        @pl.when(owner)
        def _():
            await_bytes(gram.at[step, pl.ds(0, RANK - 8)], gram_recv.at[step, 1])
            await_bytes(gram_got.at[step, pl.ds(0, ROWS // 2 - 1)], gram_send.at[step, 0])
            for side in range(2):
                await_bytes(gram_got.at[step, pl.ds(0, ROWS - 1)], gram_send.at[step, 1])
            await_bytes(gram_got.at[step, 0], gram_send.at[step, 1])

        @pl.when(jnp.logical_not(owner))
        def _():
            await_bytes(gram.at[step], gram_recv.at[step, 1])
            await_bytes(gram_got.at[step, pl.ds(0, ROWS // 2)], gram_send.at[step, 0])

        inverse_factor(gram.at[step], step == last)
        await_bytes(right_sum.at[step, pl.ds(0, RANK - 8)], right_recv.at[step, 1])
        right[...] = contract(gram[step], right_sum[step], 1, 0)
        return carry

    lax.fori_loop(0, POWER, sweep, 0)

    right_tall[...] = right[...].T
    square_own[...] = jnp.sum(right_tall[...] * right_tall[...], axis=0, keepdims=True)
    square_got[col] = square_own[...]
    for peer in col_peers:
        remote(square_own, square_got.at[col], square_send, square_recv, (row, peer))
    left[:, :HALF] = contract(gram[last], left_h[last, 0], 1, 0)
    left[:, HALF:] = contract(gram[last], left_h[last, 1], 1, 0)
    moment[...] = tall[...] - DECAY_LEFT * contract(right_tall[...], left[...], 1, 0)
    await_bytes(square_got.at[pl.ds(0, COLS - 1)], square_recv)
    norm[...] = 1.0 / (jnp.sqrt(jnp.sum(square_got[...], axis=0)) + EPSILON)

    for step in range(POWER):
        await_bytes(half_got.at[step], pair_send.at[step, 0])
        await_bytes(left_part.at[step], pair_send.at[step, 1])
        await_bytes(left_got.at[step, pl.ds(0, CHIPS - 1)], left_send.at[step, 0])
        await_bytes(left_part.at[step, pl.ds(0, HALF - 8)], left_send.at[step, 1])
        await_bytes(right_got.at[step, pl.ds(0, ROWS - 1)], right_send.at[step, 0])
        await_bytes(right_sum.at[step, pl.ds(0, RANK - 8)], right_send.at[step, 1])
    await_bytes(square_got.at[pl.ds(0, COLS - 1)], square_send)


def finish(moment, right_tall, left, norm, new_momentum, new_factor, update, factor_v, update_v, out_sem):
    stores = [pltpu.make_async_copy(moment, new_momentum, out_sem.at[0])]
    stores[0].start()
    factor_v[...] = right_tall[...] * norm[...]
    stores.append(pltpu.make_async_copy(factor_v, new_factor, out_sem.at[1]))
    stores[-1].start()
    span = WIDE // 4
    for k in range(4):
        rows = pl.ds(k * span, span)
        update_v[rows, :] = contract(factor_v[rows, :] * SCALE, left[...], 1, 0)
        stores.append(pltpu.make_async_copy(update_v.at[rows], update.at[rows], out_sem.at[k + 2]))
        stores[-1].start()
    for store in stores:
        store.wait()


def local(momentum, grads, right_factor):
    f32 = jnp.float32
    dma = pltpu.SemaphoreType.DMA
    given = (momentum.T, grads[0].T, right_factor.T)
    passed = pl.pallas_call(
        kernel,
        out_shape=(
            jax.ShapeDtypeStruct((WIDE, HIGH), f32),
            jax.ShapeDtypeStruct((WIDE, RANK), f32),
            jax.ShapeDtypeStruct((RANK, HIGH), f32),
            jax.ShapeDtypeStruct((1, RANK), f32),
        ),
        in_specs=[pl.BlockSpec(memory_space=pltpu.HBM)] * 3,
        out_specs=(pl.BlockSpec(memory_space=pltpu.VMEM),) * 4,
        scratch_shapes=[
            pltpu.VMEM((WIDE, HIGH), f32),
            pltpu.VMEM((WIDE, HIGH), jnp.bfloat16),
            pltpu.VMEM((WIDE, RANK), f32),
            pltpu.VMEM((WIDE, HIGH), f32),
            pltpu.VMEM((HIGH, WIDE), f32),
            pltpu.VMEM((RANK, WIDE), f32),
            pltpu.VMEM((POWER, RANK, HALF), f32),
            pltpu.VMEM((RANK, HALF), f32),
            pltpu.VMEM((POWER, RANK, HALF), f32),
            pltpu.VMEM((POWER, RANK, HALF), f32),
            pltpu.VMEM((POWER, CHIPS, 8, HALF), f32),
            pltpu.VMEM((POWER, 2, RANK, HALF), f32),
            pltpu.VMEM((POWER, RANK, RANK), f32),
            pltpu.VMEM((POWER, ROWS, 8, RANK), f32),
            pltpu.VMEM((POWER, RANK, RANK), f32),
            pltpu.VMEM((POWER, RANK, WIDE), f32),
            pltpu.VMEM((POWER, ROWS, 8, WIDE), f32),
            pltpu.VMEM((POWER, RANK, WIDE), f32),
            pltpu.VMEM((1, RANK), f32),
            pltpu.VMEM((COLS, 1, RANK), f32),
            dma((3,)),
            dma((POWER, 2)),
            dma((POWER, 2)),
            dma((POWER, 2)),
            dma((POWER, 3)),
            dma((POWER, 2)),
            dma((POWER, 2)),
            dma((POWER, 2)),
            dma((POWER, 2)),
            dma,
            dma,
        ],
        compiler_params=pltpu.CompilerParams(
            collective_id=0, has_side_effects=True, vmem_limit_bytes=16 << 20
        ),
    )(*(pltpu.with_memory_space_constraint(array, pltpu.HBM) for array in given))
    outs = pl.pallas_call(
        finish,
        out_shape=(
            jax.ShapeDtypeStruct((WIDE, HIGH), f32),
            jax.ShapeDtypeStruct((WIDE, RANK), f32),
            jax.ShapeDtypeStruct((WIDE, HIGH), f32),
        ),
        in_specs=[pl.BlockSpec(memory_space=pltpu.VMEM)] * 4,
        out_specs=(pl.BlockSpec(memory_space=pltpu.HBM),) * 3,
        scratch_shapes=[pltpu.VMEM((WIDE, RANK), f32), pltpu.VMEM((WIDE, HIGH), f32), dma((6,))],
        compiler_params=pltpu.CompilerParams(vmem_limit_bytes=16 << 20),
    )(*passed)
    return tuple(out.T for out in outs)


def solution(mesh):
    return jax.shard_map(
        local,
        mesh=mesh,
        in_specs=(P("row", "col"), P(None, "row", "col"), P(None, "col")),
        out_specs=(P("row", "col"), P(None, "col"), P("row", "col")),
        check_vma=False,
    )
```

```python
import jax
import jax.numpy as jnp
from jax import lax
from jax.experimental import pallas as pl
from jax.experimental.pallas import tpu as pltpu
from jax.sharding import PartitionSpec as P

M = 4096
N = 14336
RANK = 128
POWER = 2

DECAY_LEFT = 0.05
EPSILON = 1e-06
SCALE = (M * N / RANK) ** 0.5

ROWS = 16
COLS = 32
CHIPS = 16
HIGH = 256
HALF = 128
NEAR = 5
WIDE = 448
GROUP = 8
MESH = pl.DeviceIdType.MESH

HOPS = sorted((hop for hop in range(1 - CHIPS // 2, CHIPS // 2 + 1) if hop), key=lambda hop: -abs(hop))

TURNS = sorted(
    ((dy, dx) for dy in range(4) for dx in range(4) if dy or dx),
    key=lambda turn: -(min(turn[0], 4 - turn[0]) + min(turn[1], 4 - turn[1])),
)


def contract(first, second, first_dim, second_dim):
    return lax.dot_general(
        first,
        second,
        (((first_dim,), (second_dim,)), ((), ())),
        precision=lax.Precision.HIGHEST,
        preferred_element_type=jnp.float32,
    )


def spread(x):
    return jnp.broadcast_to(x, (8, RANK))


def inverse_factor(w, plain):
    lane = lax.broadcasted_iota(jnp.int32, (8, RANK), 1)
    sub = lax.broadcasted_iota(jnp.int32, (8, RANK), 0)
    count = RANK // 8
    tiles = [w[8 * i:8 * i + 8, :] for i in range(count)]
    for first in range(0, count, GROUP):
        stop = first + GROUP
        done, kept = [], []
        for k in range(first, stop):
            base = 8 * k
            tile = tiles[k]
            inside = (lane >= base) & (lane < base + 8)
            column = [jnp.where(sub >= 0, spread(tile[:, base + t:base + t + 1]), 0.0) for t in range(8)]
            d = {(i, t): spread(column[t][i:i + 1, :]) for t in range(8) for i in range(t, 8)}
            start = jnp.where(inside, jnp.where(lane - base == sub, 1.0, 0.0), tile)
            rows = [spread(start[i:i + 1, :]) for i in range(8)]
            low, scale = {}, []
            for t in range(8):
                inv = lax.rsqrt(d[t, t])
                scale.append(inv)
                for i in range(t + 1, 8):
                    low[i, t] = d[i, t] * inv
                rows[t] = rows[t] * inv
                for i in range(t + 1, 8):
                    for j in range(t + 1, i + 1):
                        d[i, j] = d[i, j] - low[i, t] * low[j, t]
                    rows[i] = rows[i] - low[i, t] * rows[t]
            block, factor = rows[0], scale[0]
            for t in range(1, 8):
                block = jnp.where(sub == t, rows[t], block)
                factor = jnp.where(sub == t, scale[t], factor)
            factor = jnp.where(plain, 1.0, jnp.sqrt(factor))
            w[base:base + 8, :] = jnp.where(lane < base + 8, block * factor, 0.0)
            done.append(block)
            kept.append(jnp.where((lane >= base + 8) & (lane < 8 * stop), 0.0, block))
            for kk in range(k + 1, stop):
                tile = tiles[kk]
                ls = []
                for t in range(8):
                    value = spread(tile[:, base + t:base + t + 1])
                    for s in range(t):
                        value = value - ls[s] * low[t, s]
                    ls.append(value * scale[t])
                tile = jnp.where(inside, 0.0, tile)
                for t in range(8):
                    tile = tile - ls[t] * rows[t]
                tiles[kk] = tile
        if stop < count:
            far = contract(jnp.concatenate(done, axis=0), jnp.concatenate(kept, axis=0), 0, 0)
            passed = (lane >= 8 * first) & (lane < 8 * stop)
            for kk in range(stop, count):
                tiles[kk] = jnp.where(passed, 0.0, tiles[kk]) - far[8 * kk:8 * kk + 8, :]


def kernel(
    momentum, grads, factor_in, moment, right_tall, left, norm,
    momentum_v, grads_v, factor_v, tall, blend, right,
    half_out, half_own, half_got, left_part, left_got, left_h,
    gram_part, gram_got, gram, right_part, right_got, right_sum, square_own, square_got,
    in_sem, pair_send, pair_recv, left_send, left_recv, gram_send, gram_recv,
    right_send, right_recv, square_send, square_recv,
):
    row = lax.axis_index("row")
    col = lax.axis_index("col")
    y, x = row // 4, row % 4
    z, core = col // 2, col % 2
    partner = (row, col + 1 - 2 * core)

    col_peers = [(col + 16 + (k + 1) // 2 * (1 if k % 2 else -1) + COLS) % COLS for k in range(31)]
    chips = [(hop, (z + hop + CHIPS) % CHIPS) for hop in HOPS]
    row_peers = [(y + dy) % 4 * 4 + (x + dx) % 4 for dy, dx in TURNS]

    barrier = pltpu.get_barrier_semaphore()
    for peer in col_peers:
        pl.semaphore_signal(barrier, inc=1, device_id=(row, peer), device_id_type=MESH)
    for peer in row_peers:
        pl.semaphore_signal(barrier, inc=1, device_id=(peer, col), device_id_type=MESH)
    for peer in row_peers:
        pl.semaphore_signal(barrier, inc=1, device_id=(peer, partner[1]), device_id_type=MESH)

    loads = [
        pltpu.make_async_copy(momentum, momentum_v, in_sem.at[0]),
        pltpu.make_async_copy(grads, grads_v, in_sem.at[1]),
        pltpu.make_async_copy(factor_in, factor_v, in_sem.at[2]),
    ]
    for load in loads:
        load.start()
    for load in loads:
        load.wait()
    tall[...] = momentum_v[...] + grads_v[...].astype(jnp.float32)
    right[...] = factor_v[...].T

    def remote(src, dst, send, recv, device):
        pltpu.make_async_remote_copy(
            src_ref=src, dst_ref=dst, send_sem=send, recv_sem=recv,
            device_id=device, device_id_type=MESH,
        ).start()

    def await_bytes(ref, sem):
        pltpu.make_async_copy(ref, ref, sem).wait()

    def piece(place):
        return pl.ds(pl.multiple_of(8 * place, 8), 8)

    owner = row % 2 == core
    last = POWER - 1

    def sweep(step, carry):
        part = contract(right[...], tall[...], 1, 0)
        first, second = part[:, :HALF], part[:, HALF:]
        half_out[step] = jnp.where(core == 0, second, first)
        half_own[...] = jnp.where(core == 0, first, second)

        @pl.when(step == 0)
        def _():
            pl.semaphore_wait(barrier, 61)

        remote(half_out.at[step], half_got.at[step], pair_send.at[step, 0], pair_recv.at[step, 0], partner)
        await_bytes(half_got.at[step], pair_recv.at[step, 0])
        left_part[step] = half_own[...] + half_got[step]
        for hop, chip in chips:
            share = left_part.at[step, piece(chip)]
            remote(share, left_got.at[step, z], left_send.at[step, 0], left_recv.at[step, 0], (row, 2 * chip + core))
        left_got[step, z] = left_part[step, piece(z)]

        @pl.when(step == 0)
        def _():
            blend[...] = tall[...].T

        await_bytes(left_got.at[step, pl.ds(0, CHIPS - 1)], left_recv.at[step, 0])
        left_h[step, core, piece(z)] = jnp.sum(left_got[step], axis=0)
        mine = left_h.at[step, core, piece(z)]
        for hop, chip in chips:
            arrival = left_recv.at[step, 1 if abs(hop) <= NEAR else 2]
            remote(mine, mine, left_send.at[step, 1], arrival, (row, 2 * chip + core))

        def forward(chip):
            share = left_h.at[step, core, piece(chip)]
            remote(share, share, pair_send.at[step, 1], pair_recv.at[step, 1], partner)

        forward(z)
        near = [chip for hop, chip in chips if abs(hop) <= NEAR]
        far = [chip for hop, chip in chips if abs(hop) > NEAR]
        await_bytes(left_part.at[step, pl.ds(0, 8 * len(near))], left_recv.at[step, 1])
        for chip in near:
            forward(chip)
        await_bytes(left_part.at[step, pl.ds(0, 8 * len(far))], left_recv.at[step, 2])
        for chip in far:
            forward(chip)
        await_bytes(left_part.at[step], pair_recv.at[step, 1])

        raw = jnp.concatenate([left_h[step, 0], left_h[step, 1]], axis=1)
        gram_part[step] = contract(raw, raw, 1, 1)
        for peer in row_peers:
            @pl.when(peer % 2 == core)
            def _():
                share = gram_part.at[step, piece(peer)]
                remote(share, gram_got.at[step, row], gram_send.at[step, 0], gram_recv.at[step, 0], (peer, col))

        right_part[step] = contract(raw, blend[...], 1, 0)
        for peer in row_peers:
            share = right_part.at[step, piece(peer)]
            remote(share, right_got.at[step, row], right_send.at[step, 0], right_recv.at[step, 0], (peer, col))

        @pl.when(owner)
        def _():
            gram_got[step, row] = gram_part[step, piece(row)]
            await_bytes(gram_got.at[step, pl.ds(0, ROWS - 1)], gram_recv.at[step, 0])
            gram[step, piece(row)] = jnp.sum(gram_got[step], axis=0)
            share = gram.at[step, piece(row)]
            for peer in row_peers:
                for side in (col, partner[1]):
                    remote(share, share, gram_send.at[step, 1], gram_recv.at[step, 1], (peer, side))
            remote(share, share, gram_send.at[step, 1], gram_recv.at[step, 1], partner)

        right_got[step, row] = right_part[step, piece(row)]
        await_bytes(right_got.at[step, pl.ds(0, ROWS - 1)], right_recv.at[step, 0])
        right_sum[step, piece(row)] = jnp.sum(right_got[step], axis=0)
        for peer in row_peers:
            share = right_sum.at[step, piece(row)]
            remote(share, share, right_send.at[step, 1], right_recv.at[step, 1], (peer, col))

        @pl.when(owner)
        def _():
            await_bytes(gram.at[step, pl.ds(0, RANK - 8)], gram_recv.at[step, 1])
            await_bytes(gram_got.at[step, pl.ds(0, ROWS // 2 - 1)], gram_send.at[step, 0])
            for side in range(2):
                await_bytes(gram_got.at[step, pl.ds(0, ROWS - 1)], gram_send.at[step, 1])
            await_bytes(gram_got.at[step, 0], gram_send.at[step, 1])

        @pl.when(jnp.logical_not(owner))
        def _():
            await_bytes(gram.at[step], gram_recv.at[step, 1])
            await_bytes(gram_got.at[step, pl.ds(0, ROWS // 2)], gram_send.at[step, 0])

        inverse_factor(gram.at[step], step == last)
        await_bytes(right_sum.at[step, pl.ds(0, RANK - 8)], right_recv.at[step, 1])
        right[...] = contract(gram[step], right_sum[step], 1, 0)
        return carry

    lax.fori_loop(0, POWER, sweep, 0)

    right_tall[...] = right[...].T
    square_own[...] = jnp.sum(right_tall[...] * right_tall[...], axis=0, keepdims=True)
    square_got[col] = square_own[...]
    for peer in col_peers:
        remote(square_own, square_got.at[col], square_send, square_recv, (row, peer))
    left[:, :HALF] = contract(gram[last], left_h[last, 0], 1, 0)
    left[:, HALF:] = contract(gram[last], left_h[last, 1], 1, 0)
    moment[...] = tall[...] - DECAY_LEFT * contract(right_tall[...], left[...], 1, 0)
    await_bytes(square_got.at[pl.ds(0, COLS - 1)], square_recv)
    norm[...] = 1.0 / (jnp.sqrt(jnp.sum(square_got[...], axis=0)) + EPSILON)

    for step in range(POWER):
        await_bytes(half_got.at[step], pair_send.at[step, 0])
        await_bytes(left_part.at[step], pair_send.at[step, 1])
        await_bytes(left_got.at[step, pl.ds(0, CHIPS - 1)], left_send.at[step, 0])
        await_bytes(left_part.at[step, pl.ds(0, HALF - 8)], left_send.at[step, 1])
        await_bytes(right_got.at[step, pl.ds(0, ROWS - 1)], right_send.at[step, 0])
        await_bytes(right_sum.at[step, pl.ds(0, RANK - 8)], right_send.at[step, 1])
    await_bytes(square_got.at[pl.ds(0, COLS - 1)], square_send)


def finish(moment, right_tall, left, norm, new_momentum, new_factor, update, factor_v, update_v, out_sem):
    stores = [pltpu.make_async_copy(moment, new_momentum, out_sem.at[0])]
    stores[0].start()
    factor_v[...] = right_tall[...] * norm[...]
    stores.append(pltpu.make_async_copy(factor_v, new_factor, out_sem.at[1]))
    stores[-1].start()
    span = WIDE // 4
    scaled = left[...] * SCALE
    left_high = scaled.astype(jnp.bfloat16)
    left_low = (scaled - left_high.astype(jnp.float32)).astype(jnp.bfloat16)
    stacked = jnp.concatenate([left_high, left_high], axis=0)
    for k in range(4):
        rows = pl.ds(k * span, span)
        part = factor_v[rows, :]
        high = part.astype(jnp.bfloat16)
        low = (part - high.astype(jnp.float32)).astype(jnp.bfloat16)
        main = jnp.dot(jnp.concatenate([high, low], axis=1), stacked, preferred_element_type=jnp.float32)
        update_v[rows, :] = main + jnp.dot(high, left_low, preferred_element_type=jnp.float32)
        stores.append(pltpu.make_async_copy(update_v.at[rows], update.at[rows], out_sem.at[k + 2]))
        stores[-1].start()
    for store in stores:
        store.wait()


def local(momentum, grads, right_factor):
    f32 = jnp.float32
    dma = pltpu.SemaphoreType.DMA
    given = (momentum.T, grads[0].T, right_factor.T)
    passed = pl.pallas_call(
        kernel,
        out_shape=(
            jax.ShapeDtypeStruct((WIDE, HIGH), f32),
            jax.ShapeDtypeStruct((WIDE, RANK), f32),
            jax.ShapeDtypeStruct((RANK, HIGH), f32),
            jax.ShapeDtypeStruct((1, RANK), f32),
        ),
        in_specs=[pl.BlockSpec(memory_space=pltpu.HBM)] * 3,
        out_specs=(pl.BlockSpec(memory_space=pltpu.VMEM),) * 4,
        scratch_shapes=[
            pltpu.VMEM((WIDE, HIGH), f32),
            pltpu.VMEM((WIDE, HIGH), jnp.bfloat16),
            pltpu.VMEM((WIDE, RANK), f32),
            pltpu.VMEM((WIDE, HIGH), f32),
            pltpu.VMEM((HIGH, WIDE), f32),
            pltpu.VMEM((RANK, WIDE), f32),
            pltpu.VMEM((POWER, RANK, HALF), f32),
            pltpu.VMEM((RANK, HALF), f32),
            pltpu.VMEM((POWER, RANK, HALF), f32),
            pltpu.VMEM((POWER, RANK, HALF), f32),
            pltpu.VMEM((POWER, CHIPS, 8, HALF), f32),
            pltpu.VMEM((POWER, 2, RANK, HALF), f32),
            pltpu.VMEM((POWER, RANK, RANK), f32),
            pltpu.VMEM((POWER, ROWS, 8, RANK), f32),
            pltpu.VMEM((POWER, RANK, RANK), f32),
            pltpu.VMEM((POWER, RANK, WIDE), f32),
            pltpu.VMEM((POWER, ROWS, 8, WIDE), f32),
            pltpu.VMEM((POWER, RANK, WIDE), f32),
            pltpu.VMEM((1, RANK), f32),
            pltpu.VMEM((COLS, 1, RANK), f32),
            dma((3,)),
            dma((POWER, 2)),
            dma((POWER, 2)),
            dma((POWER, 2)),
            dma((POWER, 3)),
            dma((POWER, 2)),
            dma((POWER, 2)),
            dma((POWER, 2)),
            dma((POWER, 2)),
            dma,
            dma,
        ],
        compiler_params=pltpu.CompilerParams(
            collective_id=0, has_side_effects=True, vmem_limit_bytes=16 << 20
        ),
    )(*(pltpu.with_memory_space_constraint(array, pltpu.HBM) for array in given))
    outs = pl.pallas_call(
        finish,
        out_shape=(
            jax.ShapeDtypeStruct((WIDE, HIGH), f32),
            jax.ShapeDtypeStruct((WIDE, RANK), f32),
            jax.ShapeDtypeStruct((WIDE, HIGH), f32),
        ),
        in_specs=[pl.BlockSpec(memory_space=pltpu.VMEM)] * 4,
        out_specs=(pl.BlockSpec(memory_space=pltpu.HBM),) * 3,
        scratch_shapes=[pltpu.VMEM((WIDE, RANK), f32), pltpu.VMEM((WIDE, HIGH), f32), dma((6,))],
        compiler_params=pltpu.CompilerParams(vmem_limit_bytes=16 << 20),
    )(*passed)
    return tuple(out.T for out in outs)


def solution(mesh):
    return jax.shard_map(
        local,
        mesh=mesh,
        in_specs=(P("row", "col"), P(None, "row", "col"), P(None, "col")),
        out_specs=(P("row", "col"), P(None, "col"), P("row", "col")),
        check_vma=False,
    )
```

```python
import jax
import jax.numpy as jnp
from jax import lax
from jax.experimental import pallas as pl
from jax.experimental.pallas import tpu as pltpu
from jax.sharding import PartitionSpec as P

M = 4096
N = 14336
RANK = 128
POWER = 2

DECAY_LEFT = 0.05
EPSILON = 1e-06
SCALE = (M * N / RANK) ** 0.5

ROWS = 16
COLS = 32
CHIPS = 16
HIGH = 256
HALF = 128
NEAR = 5
WIDE = 448
GROUP = 8
MESH = pl.DeviceIdType.MESH

HOPS = sorted((hop for hop in range(1 - CHIPS // 2, CHIPS // 2 + 1) if hop), key=lambda hop: -abs(hop))

TURNS = sorted(
    ((dy, dx) for dy in range(4) for dx in range(4) if dy or dx),
    key=lambda turn: -(min(turn[0], 4 - turn[0]) + min(turn[1], 4 - turn[1])),
)


def contract(first, second, first_dim, second_dim):
    return lax.dot_general(
        first,
        second,
        (((first_dim,), (second_dim,)), ((), ())),
        precision=lax.Precision.HIGHEST,
        preferred_element_type=jnp.float32,
    )


def spread(x):
    return jnp.broadcast_to(x, (8, RANK))


def inverse_factor(w, plain):
    lane = lax.broadcasted_iota(jnp.int32, (8, RANK), 1)
    sub = lax.broadcasted_iota(jnp.int32, (8, RANK), 0)
    count = RANK // 8
    tiles = [w[8 * i:8 * i + 8, :] for i in range(count)]
    for first in range(0, count, GROUP):
        stop = first + GROUP
        done, kept = [], []
        for k in range(first, stop):
            base = 8 * k
            tile = tiles[k]
            inside = (lane >= base) & (lane < base + 8)
            column = [jnp.where(sub >= 0, spread(tile[:, base + t:base + t + 1]), 0.0) for t in range(8)]
            d = {(i, t): spread(column[t][i:i + 1, :]) for t in range(8) for i in range(t, 8)}
            start = jnp.where(inside, jnp.where(lane - base == sub, 1.0, 0.0), tile)
            rows = [spread(start[i:i + 1, :]) for i in range(8)]
            low, scale = {}, []
            for t in range(8):
                inv = lax.rsqrt(d[t, t])
                scale.append(inv)
                for i in range(t + 1, 8):
                    low[i, t] = d[i, t] * inv
                rows[t] = rows[t] * inv
                for i in range(t + 1, 8):
                    for j in range(t + 1, i + 1):
                        d[i, j] = d[i, j] - low[i, t] * low[j, t]
                    rows[i] = rows[i] - low[i, t] * rows[t]
            block, factor = rows[0], scale[0]
            for t in range(1, 8):
                block = jnp.where(sub == t, rows[t], block)
                factor = jnp.where(sub == t, scale[t], factor)
            factor = jnp.where(plain, 1.0, jnp.sqrt(factor))
            w[base:base + 8, :] = jnp.where(lane < base + 8, block * factor, 0.0)
            done.append(block)
            kept.append(jnp.where((lane >= base + 8) & (lane < 8 * stop), 0.0, block))
            for kk in range(k + 1, stop):
                tile = tiles[kk]
                ls = []
                for t in range(8):
                    value = spread(tile[:, base + t:base + t + 1])
                    for s in range(t):
                        value = value - ls[s] * low[t, s]
                    ls.append(value * scale[t])
                tile = jnp.where(inside, 0.0, tile)
                for t in range(8):
                    tile = tile - ls[t] * rows[t]
                tiles[kk] = tile
        if stop < count:
            far = contract(jnp.concatenate(done, axis=0), jnp.concatenate(kept, axis=0), 0, 0)
            passed = (lane >= 8 * first) & (lane < 8 * stop)
            for kk in range(stop, count):
                tiles[kk] = jnp.where(passed, 0.0, tiles[kk]) - far[8 * kk:8 * kk + 8, :]


def kernel(
    momentum, grads, factor_in, moment, right_tall, left, norm,
    momentum_v, grads_v, factor_v, tall, blend, right,
    half_out, half_own, half_got, left_part, left_got, left_h,
    gram_part, gram_got, gram, right_part, right_got, right_sum, square_own, square_got,
    in_sem, pair_send, pair_recv, left_send, left_recv, gram_send, gram_recv,
    right_send, right_recv, square_send, square_recv,
):
    row = lax.axis_index("row")
    col = lax.axis_index("col")
    y, x = row // 4, row % 4
    z, core = col // 2, col % 2
    partner = (row, col + 1 - 2 * core)

    col_peers = [(col + 16 + (k + 1) // 2 * (1 if k % 2 else -1) + COLS) % COLS for k in range(31)]
    chips = [(hop, (z + hop + CHIPS) % CHIPS) for hop in HOPS]
    row_peers = [(y + dy) % 4 * 4 + (x + dx) % 4 for dy, dx in TURNS]

    barrier = pltpu.get_barrier_semaphore()
    for peer in col_peers:
        pl.semaphore_signal(barrier, inc=1, device_id=(row, peer), device_id_type=MESH)
    for peer in row_peers:
        pl.semaphore_signal(barrier, inc=1, device_id=(peer, col), device_id_type=MESH)
    for peer in row_peers:
        pl.semaphore_signal(barrier, inc=1, device_id=(peer, partner[1]), device_id_type=MESH)

    loads = [
        pltpu.make_async_copy(momentum, momentum_v, in_sem.at[0]),
        pltpu.make_async_copy(grads, grads_v, in_sem.at[1]),
        pltpu.make_async_copy(factor_in, factor_v, in_sem.at[2]),
    ]
    for load in loads:
        load.start()
    for load in loads:
        load.wait()
    tall[...] = momentum_v[...] + grads_v[...].astype(jnp.float32)
    right[...] = factor_v[...].T

    def remote(src, dst, send, recv, device):
        pltpu.make_async_remote_copy(
            src_ref=src, dst_ref=dst, send_sem=send, recv_sem=recv,
            device_id=device, device_id_type=MESH,
        ).start()

    def await_bytes(ref, sem):
        pltpu.make_async_copy(ref, ref, sem).wait()

    def piece(place):
        return pl.ds(pl.multiple_of(8 * place, 8), 8)

    owner = row % 2 == core
    last = POWER - 1

    def sweep(step, carry):
        part = contract(right[...], tall[...], 1, 0)
        first, second = part[:, :HALF], part[:, HALF:]
        half_out[step] = jnp.where(core == 0, second, first)
        half_own[...] = jnp.where(core == 0, first, second)

        @pl.when(step == 0)
        def _():
            pl.semaphore_wait(barrier, 61)

        remote(half_out.at[step], half_got.at[step], pair_send.at[step, 0], pair_recv.at[step, 0], partner)
        await_bytes(half_got.at[step], pair_recv.at[step, 0])
        left_part[step] = half_own[...] + half_got[step]
        for hop, chip in chips:
            share = left_part.at[step, piece(chip)]
            remote(share, left_got.at[step, z], left_send.at[step, 0], left_recv.at[step, 0], (row, 2 * chip + core))
        left_got[step, z] = left_part[step, piece(z)]

        @pl.when(step == 0)
        def _():
            blend[...] = tall[...].T

        await_bytes(left_got.at[step, pl.ds(0, CHIPS - 1)], left_recv.at[step, 0])
        left_h[step, core, piece(z)] = jnp.sum(left_got[step], axis=0)
        mine = left_h.at[step, core, piece(z)]
        for hop, chip in chips:
            arrival = left_recv.at[step, 1 if abs(hop) <= NEAR else 2]
            remote(mine, mine, left_send.at[step, 1], arrival, (row, 2 * chip + core))

        def forward(chip):
            share = left_h.at[step, core, piece(chip)]
            remote(share, share, pair_send.at[step, 1], pair_recv.at[step, 1], partner)

        forward(z)
        near = [chip for hop, chip in chips if abs(hop) <= NEAR]
        far = [chip for hop, chip in chips if abs(hop) > NEAR]
        await_bytes(left_part.at[step, pl.ds(0, 8 * len(near))], left_recv.at[step, 1])
        for chip in near:
            forward(chip)
        await_bytes(left_part.at[step, pl.ds(0, 8 * len(far))], left_recv.at[step, 2])
        for chip in far:
            forward(chip)
        await_bytes(left_part.at[step], pair_recv.at[step, 1])

        raw = jnp.concatenate([left_h[step, 0], left_h[step, 1]], axis=1)
        gram_part[step] = contract(raw, raw, 1, 1)
        for peer in row_peers:
            @pl.when(peer % 2 == core)
            def _():
                share = gram_part.at[step, piece(peer)]
                remote(share, gram_got.at[step, row], gram_send.at[step, 0], gram_recv.at[step, 0], (peer, col))

        right_part[step] = contract(raw, blend[...], 1, 0)
        for peer in row_peers:
            share = right_part.at[step, piece(peer)]
            remote(share, right_got.at[step, row], right_send.at[step, 0], right_recv.at[step, 0], (peer, col))

        @pl.when(owner)
        def _():
            gram_got[step, row] = gram_part[step, piece(row)]
            await_bytes(gram_got.at[step, pl.ds(0, ROWS - 1)], gram_recv.at[step, 0])
            gram[step, piece(row)] = jnp.sum(gram_got[step], axis=0)
            share = gram.at[step, piece(row)]
            for peer in row_peers:
                for side in (col, partner[1]):
                    remote(share, share, gram_send.at[step, 1], gram_recv.at[step, 1], (peer, side))
            remote(share, share, gram_send.at[step, 1], gram_recv.at[step, 1], partner)

        right_got[step, row] = right_part[step, piece(row)]
        await_bytes(right_got.at[step, pl.ds(0, ROWS - 1)], right_recv.at[step, 0])
        right_sum[step, piece(row)] = jnp.sum(right_got[step], axis=0)
        for peer in row_peers:
            share = right_sum.at[step, piece(row)]
            remote(share, share, right_send.at[step, 1], right_recv.at[step, 1], (peer, col))

        @pl.when(owner)
        def _():
            await_bytes(gram.at[step, pl.ds(0, RANK - 8)], gram_recv.at[step, 1])
            await_bytes(gram_got.at[step, pl.ds(0, ROWS // 2 - 1)], gram_send.at[step, 0])
            for side in range(2):
                await_bytes(gram_got.at[step, pl.ds(0, ROWS - 1)], gram_send.at[step, 1])
            await_bytes(gram_got.at[step, 0], gram_send.at[step, 1])

        @pl.when(jnp.logical_not(owner))
        def _():
            await_bytes(gram.at[step], gram_recv.at[step, 1])
            await_bytes(gram_got.at[step, pl.ds(0, ROWS // 2)], gram_send.at[step, 0])

        inverse_factor(gram.at[step], step == last)
        await_bytes(right_sum.at[step, pl.ds(0, RANK - 8)], right_recv.at[step, 1])
        right[...] = contract(gram[step], right_sum[step], 1, 0)
        return carry

    lax.fori_loop(0, POWER, sweep, 0)

    spot = lax.broadcasted_iota(jnp.int32, (RANK, RANK), 0) == lax.broadcasted_iota(jnp.int32, (RANK, RANK), 1)
    squares = jnp.sum(right[...] * right[...], axis=1, keepdims=True)
    square_own[...] = jnp.sum(jnp.where(spot, jnp.broadcast_to(squares, (RANK, RANK)), 0.0), axis=0, keepdims=True)
    square_got[col] = square_own[...]
    for peer in col_peers:
        remote(square_own, square_got.at[col], square_send, square_recv, (row, peer))
    right_tall[...] = right[...].T
    left[:, :HALF] = contract(gram[last], left_h[last, 0], 1, 0)
    left[:, HALF:] = contract(gram[last], left_h[last, 1], 1, 0)
    moment[...] = tall[...] - DECAY_LEFT * contract(right_tall[...], left[...], 1, 0)
    await_bytes(square_got.at[pl.ds(0, COLS - 1)], square_recv)
    norm[...] = 1.0 / (jnp.sqrt(jnp.sum(square_got[...], axis=0)) + EPSILON)

    for step in range(POWER):
        await_bytes(half_got.at[step], pair_send.at[step, 0])
        await_bytes(left_part.at[step], pair_send.at[step, 1])
        await_bytes(left_got.at[step, pl.ds(0, CHIPS - 1)], left_send.at[step, 0])
        await_bytes(left_part.at[step, pl.ds(0, HALF - 8)], left_send.at[step, 1])
        await_bytes(right_got.at[step, pl.ds(0, ROWS - 1)], right_send.at[step, 0])
        await_bytes(right_sum.at[step, pl.ds(0, RANK - 8)], right_send.at[step, 1])
    await_bytes(square_got.at[pl.ds(0, COLS - 1)], square_send)


def finish(moment, right_tall, left, norm, new_momentum, new_factor, update, factor_v, update_v, out_sem):
    stores = [pltpu.make_async_copy(moment, new_momentum, out_sem.at[0])]
    stores[0].start()
    factor_v[...] = right_tall[...] * norm[...]
    stores.append(pltpu.make_async_copy(factor_v, new_factor, out_sem.at[1]))
    stores[-1].start()
    span = WIDE // 4
    scaled = left[...] * SCALE
    left_high = scaled.astype(jnp.bfloat16)
    left_low = (scaled - left_high.astype(jnp.float32)).astype(jnp.bfloat16)
    stacked = jnp.concatenate([left_high, left_high], axis=0)
    for k in range(4):
        rows = pl.ds(k * span, span)
        part = factor_v[rows, :]
        high = part.astype(jnp.bfloat16)
        low = (part - high.astype(jnp.float32)).astype(jnp.bfloat16)
        main = jnp.dot(jnp.concatenate([high, low], axis=1), stacked, preferred_element_type=jnp.float32)
        update_v[rows, :] = main + jnp.dot(high, left_low, preferred_element_type=jnp.float32)
        stores.append(pltpu.make_async_copy(update_v.at[rows], update.at[rows], out_sem.at[k + 2]))
        stores[-1].start()
    for store in stores:
        store.wait()


def local(momentum, grads, right_factor):
    f32 = jnp.float32
    dma = pltpu.SemaphoreType.DMA
    given = (momentum.T, grads[0].T, right_factor.T)
    passed = pl.pallas_call(
        kernel,
        out_shape=(
            jax.ShapeDtypeStruct((WIDE, HIGH), f32),
            jax.ShapeDtypeStruct((WIDE, RANK), f32),
            jax.ShapeDtypeStruct((RANK, HIGH), f32),
            jax.ShapeDtypeStruct((1, RANK), f32),
        ),
        in_specs=[pl.BlockSpec(memory_space=pltpu.HBM)] * 3,
        out_specs=(pl.BlockSpec(memory_space=pltpu.VMEM),) * 4,
        scratch_shapes=[
            pltpu.VMEM((WIDE, HIGH), f32),
            pltpu.VMEM((WIDE, HIGH), jnp.bfloat16),
            pltpu.VMEM((WIDE, RANK), f32),
            pltpu.VMEM((WIDE, HIGH), f32),
            pltpu.VMEM((HIGH, WIDE), f32),
            pltpu.VMEM((RANK, WIDE), f32),
            pltpu.VMEM((POWER, RANK, HALF), f32),
            pltpu.VMEM((RANK, HALF), f32),
            pltpu.VMEM((POWER, RANK, HALF), f32),
            pltpu.VMEM((POWER, RANK, HALF), f32),
            pltpu.VMEM((POWER, CHIPS, 8, HALF), f32),
            pltpu.VMEM((POWER, 2, RANK, HALF), f32),
            pltpu.VMEM((POWER, RANK, RANK), f32),
            pltpu.VMEM((POWER, ROWS, 8, RANK), f32),
            pltpu.VMEM((POWER, RANK, RANK), f32),
            pltpu.VMEM((POWER, RANK, WIDE), f32),
            pltpu.VMEM((POWER, ROWS, 8, WIDE), f32),
            pltpu.VMEM((POWER, RANK, WIDE), f32),
            pltpu.VMEM((1, RANK), f32),
            pltpu.VMEM((COLS, 1, RANK), f32),
            dma((3,)),
            dma((POWER, 2)),
            dma((POWER, 2)),
            dma((POWER, 2)),
            dma((POWER, 3)),
            dma((POWER, 2)),
            dma((POWER, 2)),
            dma((POWER, 2)),
            dma((POWER, 2)),
            dma,
            dma,
        ],
        compiler_params=pltpu.CompilerParams(
            collective_id=0, has_side_effects=True, vmem_limit_bytes=16 << 20
        ),
    )(*(pltpu.with_memory_space_constraint(array, pltpu.HBM) for array in given))
    outs = pl.pallas_call(
        finish,
        out_shape=(
            jax.ShapeDtypeStruct((WIDE, HIGH), f32),
            jax.ShapeDtypeStruct((WIDE, RANK), f32),
            jax.ShapeDtypeStruct((WIDE, HIGH), f32),
        ),
        in_specs=[pl.BlockSpec(memory_space=pltpu.VMEM)] * 4,
        out_specs=(pl.BlockSpec(memory_space=pltpu.HBM),) * 3,
        scratch_shapes=[pltpu.VMEM((WIDE, RANK), f32), pltpu.VMEM((WIDE, HIGH), f32), dma((6,))],
        compiler_params=pltpu.CompilerParams(vmem_limit_bytes=16 << 20),
    )(*passed)
    return tuple(out.T for out in outs)


def solution(mesh):
    return jax.shard_map(
        local,
        mesh=mesh,
        in_specs=(P("row", "col"), P(None, "row", "col"), P(None, "col")),
        out_specs=(P("row", "col"), P(None, "col"), P("row", "col")),
        check_vma=False,
    )
```
